128 devices in a mesh: seq: 16 (over z, x_hi, core), exp: 8 (over y, x_lo).
Axes of the slice: x: 4 (x_hi: 2, x_lo: 2; x = x_hi * 2 + x_lo), y: 4, z: 4, core: 2. Of those that a mesh axis runs over, the one named last changes fastest.
Arguments:
- tokens: bfloat16 [524288, 1024], P(('seq', 'exp')), may hold values from -6 to 6
- norm_gain: float32 [1024], replicated, may hold values from 0.1 to 1.9
- slot_param: bfloat16 [1024, 256], replicated
- w_in: bfloat16 [64, 1024, 4096], P('exp', None, 'seq'), may hold values from -0.1875 to 0.1875
- w_out: bfloat16 [64, 4096, 1024], P('exp', 'seq'), may hold values from -0.09375 to 0.09375
Outputs:
- mixed: bfloat16 [524288, 1024], P(('seq', 'exp'))
The draws below stay inside these ranges and needn't reach their ends.
All inputs are finite; a program needn't handle non-finite values.
Results may differ from the reference program's by a relative error of at most 0.02.
The reference program's roundings to bfloat16 on the way (of `normed`, `dispatch`, `slot_in`, `hidden_act`, `slot_out` and `combine`) count: a program that leaves them out, or rounds other values in their place, can miss the bound.
Values may be sent and summed in bfloat16 or wider, within the bound.
A program may use at most 128 MiB of HBM per device.

```python
import math
import jax
import jax.numpy as jnp
from jax import lax

D = 1024
EXPERTS = 64
SLOTS_PER = 4
H = 4096
SLOTS = 256
TOKENS = 524288


def draw_slot_param(key, part):
    base = jnp.clip(jax.random.normal(key, (D, SLOTS), jnp.float32), -6.0, 6.0) * (3.0 / math.sqrt(D))
    return base.astype(jnp.bfloat16)


def steps_of(own_key, shape, cuts, least, high):
    def one(position, blocks):
        draws = jax.random.uniform(jax.random.fold_in(jax.random.fold_in(own_key, 6), position), (blocks,), jnp.float32, least / len(cuts), high / len(cuts))
        return jnp.repeat(jnp.exp(draws), shape[position] // blocks).reshape((-1,) + (1,) * (len(shape) - position - 1))

    gain = one(*cuts[0])
    for cut in cuts[1:]:
        gain = gain * one(*cut)
    return gain


def scatter_about(key, shape, deviation, reach, split=(), held_as=jnp.bfloat16):
    values = jax.random.normal(key, shape, jnp.float32) * deviation
    if len(split) > 0:
        values = steps_of(key, shape, split, -0.22, 0.18) * values
    return jnp.clip(values, min=-reach, max=reach).astype(held_as)


def setup_inputs(seed: int = 0) -> dict:
    keys = jax.random.split(jax.random.key(seed), 6)
    return {
        "tokens": scatter_about(keys[0], (TOKENS, D), 1.0, 6.0, ((0, 128),)),
        "norm_gain": jnp.clip(1.0 + 0.18 * jax.random.normal(keys[1], (D,), jnp.float32), 0.1, 1.9),
        "slot_param": draw_slot_param(jax.random.fold_in(keys[5], 71), 0),
        "w_in": scatter_about(keys[3], (EXPERTS, D, H), D ** -0.5, 0.1875, ((0, 8), (2, 16))),
        "w_out": scatter_about(keys[4], (EXPERTS, H, D), H ** -0.5, 0.09375, ((0, 8), (1, 16))),
    }


def normalize(rows, norm_gain):
    values = rows.astype(jnp.float32)
    scale = lax.rsqrt(lax.optimization_barrier(jnp.mean(values * values, axis=1, keepdims=True)) + 1e-06)
    return (values * scale * norm_gain[None, :]).astype(jnp.bfloat16)

def reference(tokens, norm_gain, slot_param, w_in, w_out):
    blocks = 64
    rows = tokens.shape[0] // blocks
    stacked = tokens.reshape(blocks, rows, D)

    def block_logits(block):
        normed = normalize(block, norm_gain)
        return (normed, jnp.dot(normed, slot_param, preferred_element_type=jnp.float32))

    def peak_of(block):
        return lax.optimization_barrier(jnp.max(block_logits(block)[1], axis=0))
    col_peak = lax.optimization_barrier(jnp.max(lax.map(peak_of, stacked), axis=0))

    def accumulate(carry, block):
        normed, logits = block_logits(block)
        raw = jnp.exp(logits - col_peak[None, :])
        dispatch = raw.astype(jnp.bfloat16)
        part = lax.dot_general(dispatch, normed, (((0,), (0,)), ((), ())), preferred_element_type=jnp.float32)
        return ((carry[0] + part, carry[1] + lax.optimization_barrier(jnp.sum(raw, axis=0))), None)
    start = (jnp.zeros((SLOTS, D), jnp.float32), jnp.zeros((SLOTS,), jnp.float32))
    (weighted, col_total), unused = lax.scan(accumulate, start, stacked)
    slot_in = (weighted / col_total[:, None]).astype(jnp.bfloat16).reshape(EXPERTS, SLOTS_PER, D)

    def expert(index):
        first = jnp.dot(slot_in[index], w_in[index], preferred_element_type=jnp.float32)
        hidden_act = jax.nn.gelu(first, approximate=False).astype(jnp.bfloat16)
        return jnp.dot(hidden_act, w_out[index], preferred_element_type=jnp.float32).astype(jnp.bfloat16)
    slot_out = lax.map(expert, jnp.arange(EXPERTS, dtype=jnp.int32)).reshape(SLOTS, D)

    def output_of(block):
        logits = block_logits(block)[1]
        combine = jax.nn.softmax(logits, axis=1).astype(jnp.bfloat16)
        return jnp.dot(combine, slot_out, preferred_element_type=jnp.float32).astype(jnp.bfloat16)
    return lax.map(output_of, stacked).reshape(tokens.shape[0], D)
```

```python
import functools

import jax
import jax.numpy as jnp
from jax import lax
from jax.experimental import pallas as pl
from jax.experimental.pallas import tpu as pltpu
from jax.sharding import PartitionSpec as P

MESH = pl.DeviceIdType.MESH
F32 = jnp.float32
BF16 = jnp.bfloat16
PLANE = 16
COLUMN = 8
META = 128


def split3(v):
    hi = v.astype(BF16).astype(F32)
    rest = v - hi
    mid = rest.astype(BF16).astype(F32)
    return hi, mid, rest - mid


def meta_block(peak, total):
    rows = peak.shape[0]
    lane = lax.broadcasted_iota(jnp.int32, (rows, META), 1)
    out = jnp.zeros((rows, META), F32)
    for i, part in enumerate(split3(peak) + split3(total)):
        out = jnp.where(lane == i, part, out)
    return out.astype(BF16)


def read_meta(block):
    v = block.astype(F32)
    peak = v[:, 0:1] + v[:, 1:2] + v[:, 2:3]
    total = v[:, 3:4] + v[:, 4:5] + v[:, 5:6]
    return peak, total


def moe_kernel(
    tok, gain_ref, slot_ref, win_hbm, wout_hbm,
    comb_hbm, g_ref,
    xbuf, lbuf, dbuf, cbuf, win, wout, mx, acc, colbuf,
    s0, r0, s1, r1, s2, r2, sl, hbuf, xs, xr, s4, r4,
    tsem, wsem, csem,
    core_send, core_recv, plane_send, plane_recv, column_send, column_recv,
    back_send, back_recv, gather_send, gather_recv, fwd_send, fwd_recv,
):
    tokens, width = xbuf.shape
    slots = slot_ref.shape[1]
    half = width // 2
    group = sl.shape[1]
    piece = group // 2
    local_experts = win.shape[0]
    per = group // local_experts
    hidden = win.shape[2]
    chunks = tsem.shape[0]
    rows = tokens // chunks

    s = lax.axis_index("seq")
    e = lax.axis_index("exp")
    c = lax.rem(s, 2)
    xh = lax.rem(s // 2, 2)
    z0 = lax.rem(s // 4, 2)
    z1 = s // 8
    xl = lax.rem(e, 2)
    y0 = lax.rem(e // 2, 2)
    y1 = e // 4

    def bit(b, k, i):
        return 1 - b if (k >> i) & 1 else b

    def plane_peer(k):
        pe = (bit(y1, k, 2) * 2 + bit(y0, k, 1)) * 2 + bit(xl, k, 0)
        ph = bit(xh, k, 3)
        ps = ((z1 * 2 + z0) * 2 + ph) * 2 + c
        row = pl.multiple_of(pe * group + ph * piece, piece)
        return (ps, pe), row

    def column_peer(k):
        ps = ((bit(z1, k, 2) * 2 + bit(z0, k, 1)) * 2 + bit(xh, k, 0)) * 2 + c
        return (ps, e)

    partner = (s + 1 - 2 * c, e)

    def remote(src, dst, send, recv, device):
        return pltpu.make_async_remote_copy(
            src_ref=src, dst_ref=dst, send_sem=send, recv_sem=recv,
            device_id=device, device_id_type=MESH,
        )

    def token_copy(i):
        at = pl.ds(pl.multiple_of(i * rows, rows), rows)
        return pltpu.make_async_copy(tok.at[at], xbuf.at[at], tsem.at[i])

    for i in range(chunks):
        token_copy(i).start()
    barrier = pltpu.get_barrier_semaphore()
    greeted = [partner]
    greeted += [plane_peer(k)[0] for k in range(1, PLANE)]
    greeted += [column_peer(k) for k in range(2, COLUMN)]
    for device in greeted:
        pl.semaphore_signal(barrier, inc=1, device_id=device, device_id_type=MESH)
    win_copy = pltpu.make_async_copy(win_hbm, win, wsem.at[0])
    wout_copy = pltpu.make_async_copy(wout_hbm, wout, wsem.at[1])

    gain = gain_ref[...]
    mx[...] = jnp.full(mx.shape, -jnp.inf, F32)

    @pl.loop(0, chunks)
    def _(i):
        token_copy(i).wait()
        base = i * rows

        @pl.loop(0, rows // 32, unroll=4)
        def _(j):
            at = pl.ds(pl.multiple_of(base + j * 32, 32), 32)
            v = xbuf[at, :].astype(F32)
            scale = lax.rsqrt(jnp.mean(v * v, axis=1, keepdims=True) + 1e-06)
            xbuf[at, :] = (v * scale * gain).astype(BF16)

        at = pl.ds(pl.multiple_of(base, rows), rows)
        logits = jnp.dot(xbuf[at, :], slot_ref[...], preferred_element_type=F32)
        lbuf[at, :] = logits
        mx[...] = jnp.maximum(mx[...], jnp.max(logits.reshape(rows // 8, 8, slots), axis=0))

    win_copy.start()
    wout_copy.start()
    peak = jnp.max(mx[...], axis=0, keepdims=True)

    def dispatch(i, total):
        at = pl.ds(pl.multiple_of(i * 64, 64), 64)
        raw = jnp.exp(lbuf[at, :] - peak)
        dbuf[at, :] = raw.astype(BF16)
        return total + jnp.sum(raw.reshape(8, 8, slots), axis=0)

    total = lax.fori_loop(0, tokens // 64, dispatch, jnp.zeros((8, slots), F32), unroll=4)
    total = jnp.sum(total, axis=0, keepdims=True)
    line = lax.broadcasted_iota(jnp.int32, (META, slots), 0)
    both = jnp.where(line == 0, peak, jnp.where(line == 1, total, 0.0))
    colbuf[...] = jnp.transpose(both)
    my_meta = meta_block(colbuf[:, 0:1], colbuf[:, 1:2])

    depth = 1024 if tokens % 1024 == 0 else tokens

    def weigh(h):
        acc[...] = jnp.zeros(acc.shape, F32)
        cols = pl.ds(pl.multiple_of(h * half, half), half)

        @pl.loop(0, tokens // depth)
        def _(i):
            at = pl.ds(pl.multiple_of(i * depth, depth), depth)
            acc[...] += lax.dot_general(
                dbuf[at, :], xbuf[at, cols], (((0,), (0,)), ((), ())),
                preferred_element_type=F32,
            )

    pl.semaphore_wait(barrier, len(greeted))
    weigh(1 - c)
    s0[:, :half] = acc[...].astype(BF16)
    s0[:, half:] = my_meta
    first_copy = remote(s0, r0, core_send.at[0], core_recv.at[0], partner)
    first_copy.start()
    weigh(c)
    first_copy.wait()

    def chip_piece(row):
        at = pl.ds(row, piece)
        mine, my_total = colbuf[at, 0:1], colbuf[at, 1:2]
        other, other_total = read_meta(r0[at, half:])
        joint = jnp.maximum(mine, other)
        wa, wb = jnp.exp(mine - joint), jnp.exp(other - joint)
        s1[at, :half] = (acc[at, :] * wa + r0[at, :half].astype(F32) * wb).astype(BF16)
        s1[at, half:] = meta_block(joint, my_total * wa + other_total * wb)

    order = sorted(range(1, PLANE), key=lambda k: -bin(k).count("1"))
    plane_copies = {}
    for k in order:
        device, row = plane_peer(k)
        chip_piece(row)
        at = pl.ds(row, piece)
        plane_copies[k] = remote(s1.at[at], r1.at[k], plane_send.at[k], plane_recv.at[k], device)
        plane_copies[k].start()
    my_row = plane_peer(0)[1]
    chip_piece(my_row)

    @pl.loop(0, tokens // 32, unroll=4)
    def _(i):
        at = pl.ds(pl.multiple_of(i * 32, 32), 32)
        v = lbuf[at, :]
        ex = jnp.exp(v - jnp.max(v, axis=1, keepdims=True))
        cbuf[at, :] = (ex / jnp.sum(ex, axis=1, keepdims=True)).astype(BF16)

    comb_copy = pltpu.make_async_copy(cbuf, comb_hbm, csem.at[0])
    comb_copy.start()

    def merge(blocks):
        metas = [read_meta(b[:, half:]) for b in blocks]
        joint = functools.reduce(jnp.maximum, [m for m, _ in metas])
        scales = [jnp.exp(m - joint) for m, _ in metas]
        out = sum(b[:, :half].astype(F32) * w for b, w in zip(blocks, scales))
        return out, joint, sum(t * w for (_, t), w in zip(metas, scales))

    for k in order:
        plane_copies[k].wait_recv()
    summed, joint, total_k = merge([s1[pl.ds(my_row, piece), :]] + [r1[k] for k in range(1, PLANE)])
    s2[:, :half] = summed.astype(BF16)
    s2[:, half:] = meta_block(joint, total_k)

    column_copies = {}
    for k in sorted(range(1, COLUMN), key=lambda k: -bin(k).count("1")):
        column_copies[k] = remote(s2, r2.at[k], column_send.at[k], column_recv.at[k], column_peer(k))
        column_copies[k].start()
    for k in range(1, COLUMN):
        column_copies[k].wait_recv()
    for odd in range(2):
        blocks = [s2[...] if k == 0 else r2[k] for k in range(odd, COLUMN, 2)]
        out, _, tot = merge(blocks)
        at = pl.multiple_of((1 - xh if odd else xh) * piece, piece)
        sl[c, pl.ds(at, piece), :] = (out / tot).astype(BF16)
    in_copy = remote(sl.at[c], sl.at[c], core_send.at[1], core_recv.at[1], partner)
    in_copy.start()
    win_copy.wait()
    wout_copy.wait()
    in_copy.wait()

    owner = lax.broadcasted_iota(jnp.int32, (group, hidden), 0) // per
    first = jnp.zeros((group, hidden), F32)
    for x in range(local_experts):
        y = jnp.dot(sl[0], win[x, :half, :], preferred_element_type=F32)
        y += jnp.dot(sl[1], win[x, half:, :], preferred_element_type=F32)
        first = jnp.where(owner == x, y, first)
    act = 0.5 * first * (1.0 + lax.erf(first * 0.7071067811865476))
    for x in range(local_experts):
        hbuf[:, x * hidden:(x + 1) * hidden] = jnp.where(owner == x, act, 0.0).astype(BF16)

    def project(h):
        cols = pl.ds(pl.multiple_of(h * half, half), half)
        return sum(
            jnp.dot(hbuf[:, x * hidden:(x + 1) * hidden], wout[x, :, cols], preferred_element_type=F32)
            for x in range(local_experts)
        )

    xs[...] = project(1 - c).astype(BF16)
    out_copy = remote(xs, xr, core_send.at[2], core_recv.at[2], partner)
    out_copy.start()
    own = project(c)
    out_copy.wait()
    s4[...] = (own + xr[...].astype(F32)).astype(BF16)

    back_copies = {}
    for k in sorted(range(1, COLUMN), key=lambda k: -bin(k).count("1")):
        at = pl.ds(pl.multiple_of(bit(xh, k, 0) * piece, piece), piece)
        back_copies[k] = remote(s4.at[at], r4.at[k], back_send.at[k], back_recv.at[k], column_peer(k))
        back_copies[k].start()
    mine = s4[pl.ds(pl.multiple_of(xh * piece, piece), piece), :].astype(F32)
    for k in range(1, COLUMN):
        back_copies[k].wait_recv()
        mine += r4[k].astype(F32)
    at = pl.ds(my_row, piece)
    g_ref[c, at, :] = mine.astype(BF16)

    gathers = {}
    for k in order:
        gathers[k] = remote(
            g_ref.at[c, at], g_ref.at[c, at], gather_send.at[k], gather_recv.at[k], plane_peer(k)[0]
        )
        gathers[k].start()
    forwards = []
    for k in [0] + order[::-1]:
        if k:
            gathers[k].wait_recv()
        there = pl.ds(plane_peer(k)[1], piece)
        forwards.append(
            remote(g_ref.at[c, there], g_ref.at[c, there], fwd_send.at[k], fwd_recv.at[k], partner)
        )
        forwards[-1].start()
    for copy in forwards:
        copy.wait()
    for copies in (plane_copies, column_copies, back_copies, gathers):
        for copy in copies.values():
            copy.wait_send()
    comb_copy.wait()


def mix_kernel(c_ref, g_ref, o_ref):
    half = g_ref.shape[2]
    for h in range(2):
        o_ref[:, h * half:(h + 1) * half] = jnp.dot(
            c_ref[...], g_ref[h], preferred_element_type=F32
        ).astype(BF16)


def on_device(tokens, norm_gain, slot_param, w_in, w_out):
    n, width = tokens.shape
    slots = slot_param.shape[1]
    half = width // 2
    group = slots // lax.axis_size("exp")
    piece = group // 2
    hidden = w_in.shape[2]
    chunks = 8
    wide = half + META
    dma = pltpu.SemaphoreType.DMA
    anywhere = pl.BlockSpec(memory_space=pl.ANY)
    vmem = pl.BlockSpec(memory_space=pltpu.VMEM)
    combine, gathered = pl.pallas_call(
        moe_kernel,
        out_shape=(
            jax.ShapeDtypeStruct((n, slots), BF16),
            jax.ShapeDtypeStruct((2, slots, half), BF16),
        ),
        in_specs=[anywhere, vmem, vmem, anywhere, anywhere],
        out_specs=(anywhere, vmem),
        scratch_shapes=[
            pltpu.VMEM((n, width), BF16),
            pltpu.VMEM((n, slots), F32),
            pltpu.VMEM((n, slots), BF16),
            pltpu.VMEM((n, slots), BF16),
            pltpu.VMEM(w_in.shape, BF16),
            pltpu.VMEM(w_out.shape, BF16),
            pltpu.VMEM((8, slots), F32),
            pltpu.VMEM((slots, half), F32),
            pltpu.VMEM((slots, META), F32),
            pltpu.VMEM((slots, wide), BF16),
            pltpu.VMEM((slots, wide), BF16),
            pltpu.VMEM((slots, wide), BF16),
            pltpu.VMEM((PLANE, piece, wide), BF16),
            pltpu.VMEM((piece, wide), BF16),
            pltpu.VMEM((COLUMN, piece, wide), BF16),
            pltpu.VMEM((2, group, half), BF16),
            pltpu.VMEM((group, w_in.shape[0] * hidden), BF16),
            pltpu.VMEM((group, half), BF16),
            pltpu.VMEM((group, half), BF16),
            pltpu.VMEM((group, half), BF16),
            pltpu.VMEM((COLUMN, piece, half), BF16),
            dma((chunks,)),
            dma((2,)),
            dma((1,)),
            dma((3,)), dma((3,)),
            dma((PLANE,)), dma((PLANE,)),
            dma((COLUMN,)), dma((COLUMN,)),
            dma((COLUMN,)), dma((COLUMN,)),
            dma((PLANE,)), dma((PLANE,)),
            dma((PLANE,)), dma((PLANE,)),
        ],
        compiler_params=pltpu.CompilerParams(
            collective_id=0, has_side_effects=True, vmem_limit_bytes=48 * 2**20
        ),
        name="moe",
    )(tokens, norm_gain.reshape(1, width), slot_param, w_in, w_out)
    block = n // 8
    return pl.pallas_call(
        mix_kernel,
        grid=(8,),
        out_shape=jax.ShapeDtypeStruct((n, width), BF16),
        in_specs=[
            pl.BlockSpec((block, slots), lambda i: (i, 0)),
            pl.BlockSpec((2, slots, half), lambda i: (0, 0, 0)),
        ],
        out_specs=pl.BlockSpec((block, width), lambda i: (i, 0)),
        name="mix",
    )(combine, gathered)


def solution(mesh):
    in_specs = (P(("seq", "exp"), None), P(), P(), P("exp", None, "seq"), P("exp", "seq", None))
    out_specs = P(("seq", "exp"), None)
    return jax.shard_map(
        on_device, mesh=mesh, in_specs=in_specs, out_specs=out_specs, check_vma=False
    )
```

```python
import functools

import jax
import jax.numpy as jnp
from jax import lax
from jax.experimental import pallas as pl
from jax.experimental.pallas import tpu as pltpu
from jax.sharding import PartitionSpec as P

MESH = pl.DeviceIdType.MESH
F32 = jnp.float32
BF16 = jnp.bfloat16
PLANE = 16
COLUMN = 8
META = 128


def split3(v):
    hi = v.astype(BF16).astype(F32)
    rest = v - hi
    mid = rest.astype(BF16).astype(F32)
    return hi, mid, rest - mid


def meta_block(peak, total):
    rows = peak.shape[0]
    lane = lax.broadcasted_iota(jnp.int32, (rows, META), 1)
    out = jnp.zeros((rows, META), F32)
    for i, part in enumerate(split3(peak) + split3(total)):
        out = jnp.where(lane == i, part, out)
    return out.astype(BF16)


def read_meta(block):
    v = block.astype(F32)
    peak = v[:, 0:1] + v[:, 1:2] + v[:, 2:3]
    total = v[:, 3:4] + v[:, 4:5] + v[:, 5:6]
    return peak, total


def moe_kernel(
    tok, gain_hbm, slot_hbm, win_hbm, wout_hbm,
    cbuf, g_ref,
    raw, xbuf, pair, lbuf, dbuf, win, wout, gain_ref, slot_ref, mx, acc, colbuf,
    s0, r0, s1, r1, s2, r2, sl, hbuf, xs, xr, s4, r4,
    tsem, wsem,
    core_send, core_recv, plane_send, plane_recv, column_send, column_recv,
    back_send, back_recv, gather_send, gather_recv, fwd_send, fwd_recv,
):
    tokens, width = xbuf.shape
    slots = slot_ref.shape[1]
    half = width // 2
    group = sl.shape[1]
    piece = group // 2
    local_experts = win.shape[0]
    per = group // local_experts
    hidden = win.shape[2]
    chunks = tsem.shape[0]
    rows = tokens // chunks

    s = lax.axis_index("seq")
    e = lax.axis_index("exp")
    c = lax.rem(s, 2)
    xh = lax.rem(s // 2, 2)
    z0 = lax.rem(s // 4, 2)
    z1 = s // 8
    xl = lax.rem(e, 2)
    y0 = lax.rem(e // 2, 2)
    y1 = e // 4

    def bit(b, k, i):
        return 1 - b if (k >> i) & 1 else b

    def plane_peer(k):
        pe = (bit(y1, k, 2) * 2 + bit(y0, k, 1)) * 2 + bit(xl, k, 0)
        ph = bit(xh, k, 3)
        ps = ((z1 * 2 + z0) * 2 + ph) * 2 + c
        row = pl.multiple_of(pe * group + ph * piece, piece)
        return (ps, pe), row

    def column_peer(k):
        ps = ((bit(z1, k, 2) * 2 + bit(z0, k, 1)) * 2 + bit(xh, k, 0)) * 2 + c
        return (ps, e)

    partner = (s + 1 - 2 * c, e)

    def remote(src, dst, send, recv, device):
        return pltpu.make_async_remote_copy(
            src_ref=src, dst_ref=dst, send_sem=send, recv_sem=recv,
            device_id=device, device_id_type=MESH,
        )

    def token_copy(i):
        at = pl.ds(pl.multiple_of(i * rows, rows), rows)
        return pltpu.make_async_copy(tok.at[at], raw.at[at], tsem.at[i])

    token_copy(0).start()
    gain_copy = pltpu.make_async_copy(gain_hbm, gain_ref, wsem.at[2])
    slot_copy = pltpu.make_async_copy(slot_hbm, slot_ref, wsem.at[3])
    gain_copy.start()
    slot_copy.start()
    for i in range(1, chunks):
        token_copy(i).start()
    barrier = pltpu.get_barrier_semaphore()
    greeted = [partner]
    greeted += [plane_peer(k)[0] for k in range(1, PLANE)]
    greeted += [column_peer(k) for k in range(2, COLUMN)]
    for device in greeted:
        pl.semaphore_signal(barrier, inc=1, device_id=device, device_id_type=MESH)
    win_copy = pltpu.make_async_copy(win_hbm, win, wsem.at[0])
    wout_copy = pltpu.make_async_copy(wout_hbm, wout, wsem.at[1])

    gain_copy.wait()
    slot_copy.wait()
    gain = gain_ref[...]
    mx[...] = jnp.full(mx.shape, -jnp.inf, F32)

    def norm(i, slot):
        for q in range(rows // 32):
            at = pl.ds(pl.multiple_of(i * rows + q * 32, 32), 32)
            v = raw[at, :].astype(F32)
            scale = lax.rsqrt(jnp.mean(v * v, axis=1, keepdims=True) + 1e-06)
            normed = (v * scale * gain).astype(BF16)
            xbuf[at, :] = normed
            pair[slot][q * 32:(q + 1) * 32, :] = normed

    def project_slots(i, slot):
        at = pl.ds(pl.multiple_of(i * rows, rows), rows)
        logits = jnp.dot(pair[slot][...], slot_ref[...], preferred_element_type=F32)
        lbuf[at, :] = logits
        mx[...] = jnp.maximum(mx[...], jnp.max(logits.reshape(rows // 8, 8, slots), axis=0))

    token_copy(0).wait()
    norm(0, 0)

    @pl.loop(0, chunks // 2 - 1)
    def _(i):
        for slot in range(2):
            token_copy(2 * i + slot + 1).wait()
            norm(2 * i + slot + 1, 1 - slot)
            project_slots(2 * i + slot, slot)

    token_copy(chunks - 1).wait()
    norm(chunks - 1, 1)
    project_slots(chunks - 2, 0)
    project_slots(chunks - 1, 1)

    win_copy.start()
    wout_copy.start()
    peak = jnp.max(mx[...], axis=0, keepdims=True)

    step = min(256, tokens)

    def dispatch(i, total):
        at = pl.ds(pl.multiple_of(i * step, step), step)
        ex = jnp.exp(lbuf[at, :] - peak)
        dbuf[at, :] = ex.astype(BF16)
        return total + jnp.sum(ex.reshape(step // 8, 8, slots), axis=0)

    total = lax.fori_loop(0, tokens // step, dispatch, jnp.zeros((8, slots), F32))
    total = jnp.sum(total, axis=0, keepdims=True)
    line = lax.broadcasted_iota(jnp.int32, (META, slots), 0)
    both = jnp.where(line == 0, peak, jnp.where(line == 1, total, 0.0))
    colbuf[...] = jnp.transpose(both)
    my_meta = meta_block(colbuf[:, 0:1], colbuf[:, 1:2])

    def weigh(h):
        cols = pl.ds(pl.multiple_of(h * half, half), half)
        return lax.dot_general(
            dbuf[...], xbuf[:, cols], (((0,), (0,)), ((), ())), preferred_element_type=F32
        )

    s0[:, :half] = weigh(1 - c).astype(BF16)
    s0[:, half:] = my_meta
    pl.semaphore_wait(barrier, len(greeted))
    first_copy = remote(s0, r0, core_send.at[0], core_recv.at[0], partner)
    first_copy.start()
    acc[...] = weigh(c)
    first_copy.wait()

    def chip_piece(row):
        at = pl.ds(row, piece)
        mine, my_total = colbuf[at, 0:1], colbuf[at, 1:2]
        other, other_total = read_meta(r0[at, half:])
        joint = jnp.maximum(mine, other)
        wa, wb = jnp.exp(mine - joint), jnp.exp(other - joint)
        s1[at, :half] = (acc[at, :] * wa + r0[at, :half].astype(F32) * wb).astype(BF16)
        s1[at, half:] = meta_block(joint, my_total * wa + other_total * wb)

    order = sorted(range(1, PLANE), key=lambda k: -bin(k).count("1"))
    plane_copies = {}
    for k in order:
        device, row = plane_peer(k)
        chip_piece(row)
        at = pl.ds(row, piece)
        plane_copies[k] = remote(s1.at[at], r1.at[k], plane_send.at[k], plane_recv.at[k], device)
        plane_copies[k].start()
    my_row = plane_peer(0)[1]
    chip_piece(my_row)

    @pl.loop(0, tokens // step, unroll=2)
    def _(i):
        at = pl.ds(pl.multiple_of(i * step, step), step)
        v = lbuf[at, :]
        ex = jnp.exp(v - jnp.max(v, axis=1, keepdims=True))
        cbuf[at, :] = (ex * (1.0 / jnp.sum(ex, axis=1, keepdims=True))).astype(BF16)

    def merge(blocks):
        metas = [read_meta(b[:, half:]) for b in blocks]
        joint = functools.reduce(jnp.maximum, [m for m, _ in metas])
        scales = [jnp.exp(m - joint) for m, _ in metas]
        out = sum(b[:, :half].astype(F32) * w for b, w in zip(blocks, scales))
        return out, joint, sum(t * w for (_, t), w in zip(metas, scales))

    for k in order:
        plane_copies[k].wait_recv()
    summed, joint, total_k = merge([s1[pl.ds(my_row, piece), :]] + [r1[k] for k in range(1, PLANE)])
    s2[:, :half] = summed.astype(BF16)
    s2[:, half:] = meta_block(joint, total_k)

    column_copies = {}
    for k in sorted(range(1, COLUMN), key=lambda k: -bin(k).count("1")):
        column_copies[k] = remote(s2, r2.at[k], column_send.at[k], column_recv.at[k], column_peer(k))
        column_copies[k].start()
    for k in range(1, COLUMN):
        column_copies[k].wait_recv()
    for odd in range(2):
        blocks = [s2[...] if k == 0 else r2[k] for k in range(odd, COLUMN, 2)]
        out, _, tot = merge(blocks)
        at = pl.multiple_of((1 - xh if odd else xh) * piece, piece)
        sl[c, pl.ds(at, piece), :] = (out / tot).astype(BF16)
    in_copy = remote(sl.at[c], sl.at[c], core_send.at[1], core_recv.at[1], partner)
    in_copy.start()
    win_copy.wait()
    wout_copy.wait()
    in_copy.wait()

    owner = lax.broadcasted_iota(jnp.int32, (group, hidden), 0) // per
    first = jnp.zeros((group, hidden), F32)
    for x in range(local_experts):
        y = jnp.dot(sl[0], win[x, :half, :], preferred_element_type=F32)
        y += jnp.dot(sl[1], win[x, half:, :], preferred_element_type=F32)
        first = jnp.where(owner == x, y, first)
    act = 0.5 * first * (1.0 + lax.erf(first * 0.7071067811865476))
    for x in range(local_experts):
        hbuf[:, x * hidden:(x + 1) * hidden] = jnp.where(owner == x, act, 0.0).astype(BF16)

    def project(h):
        cols = pl.ds(pl.multiple_of(h * half, half), half)
        return sum(
            jnp.dot(hbuf[:, x * hidden:(x + 1) * hidden], wout[x, :, cols], preferred_element_type=F32)
            for x in range(local_experts)
        )

    xs[...] = project(1 - c).astype(BF16)
    out_copy = remote(xs, xr, core_send.at[2], core_recv.at[2], partner)
    out_copy.start()
    own = project(c)
    out_copy.wait()
    s4[...] = (own + xr[...].astype(F32)).astype(BF16)

    back_copies = {}
    for k in sorted(range(1, COLUMN), key=lambda k: -bin(k).count("1")):
        at = pl.ds(pl.multiple_of(bit(xh, k, 0) * piece, piece), piece)
        back_copies[k] = remote(s4.at[at], r4.at[k], back_send.at[k], back_recv.at[k], column_peer(k))
        back_copies[k].start()
    mine = s4[pl.ds(pl.multiple_of(xh * piece, piece), piece), :].astype(F32)
    for k in range(1, COLUMN):
        back_copies[k].wait_recv()
        mine += r4[k].astype(F32)
    at = pl.ds(my_row, piece)
    g_ref[c, at, :] = mine.astype(BF16)

    gathers = {}
    for k in order:
        gathers[k] = remote(
            g_ref.at[c, at], g_ref.at[c, at], gather_send.at[k], gather_recv.at[k], plane_peer(k)[0]
        )
        gathers[k].start()
    forwards = []
    for k in [0] + order[::-1]:
        if k:
            gathers[k].wait_recv()
        there = pl.ds(plane_peer(k)[1], piece)
        forwards.append(
            remote(g_ref.at[c, there], g_ref.at[c, there], fwd_send.at[k], fwd_recv.at[k], partner)
        )
        forwards[-1].start()
    for copy in forwards:
        copy.wait()
    for copies in (plane_copies, column_copies, back_copies, gathers):
        for copy in copies.values():
            copy.wait_send()


def mix_kernel(c_ref, g_ref, o_hbm, obuf, sem):
    half = g_ref.shape[2]
    blocks = sem.shape[0]
    rows = obuf.shape[0] // blocks
    copies = []
    for i in range(blocks):
        at = pl.ds(i * rows, rows)
        for h in range(2):
            obuf[at, h * half:(h + 1) * half] = jnp.dot(
                c_ref[at, :], g_ref[h], preferred_element_type=F32
            ).astype(BF16)
        copies.append(pltpu.make_async_copy(obuf.at[at], o_hbm.at[at], sem.at[i]))
        copies[-1].start()
    for copy in copies:
        copy.wait()


def on_device(tokens, norm_gain, slot_param, w_in, w_out):
    n, width = tokens.shape
    slots = slot_param.shape[1]
    half = width // 2
    group = slots // lax.axis_size("exp")
    piece = group // 2
    hidden = w_in.shape[2]
    chunks = 8
    wide = half + META
    dma = pltpu.SemaphoreType.DMA
    anywhere = pl.BlockSpec(memory_space=pl.ANY)
    vmem = pl.BlockSpec(memory_space=pltpu.VMEM)
    combine, gathered = pl.pallas_call(
        moe_kernel,
        out_shape=(
            pltpu.VMEM((n, slots), BF16),
            pltpu.VMEM((2, slots, half), BF16),
        ),
        in_specs=[anywhere] * 5,
        out_specs=(vmem, vmem),
        scratch_shapes=[
            pltpu.VMEM((n, width), BF16),
            pltpu.VMEM((n, width), BF16),
            [pltpu.VMEM((n // chunks, width), BF16)] * 2,
            pltpu.VMEM((n, slots), F32),
            pltpu.VMEM((n, slots), BF16),
            pltpu.VMEM(w_in.shape, BF16),
            pltpu.VMEM(w_out.shape, BF16),
            pltpu.VMEM((1, width), F32),
            pltpu.VMEM((width, slots), BF16),
            pltpu.VMEM((8, slots), F32),
            pltpu.VMEM((slots, half), F32),
            pltpu.VMEM((slots, META), F32),
            pltpu.VMEM((slots, wide), BF16),
            pltpu.VMEM((slots, wide), BF16),
            pltpu.VMEM((slots, wide), BF16),
            pltpu.VMEM((PLANE, piece, wide), BF16),
            pltpu.VMEM((piece, wide), BF16),
            pltpu.VMEM((COLUMN, piece, wide), BF16),
            pltpu.VMEM((2, group, half), BF16),
            pltpu.VMEM((group, w_in.shape[0] * hidden), BF16),
            pltpu.VMEM((group, half), BF16),
            pltpu.VMEM((group, half), BF16),
            pltpu.VMEM((group, half), BF16),
            pltpu.VMEM((COLUMN, piece, half), BF16),
            dma((chunks,)),
            dma((4,)),
            dma((3,)), dma((3,)),
            dma((PLANE,)), dma((PLANE,)),
            dma((COLUMN,)), dma((COLUMN,)),
            dma((COLUMN,)), dma((COLUMN,)),
            dma((PLANE,)), dma((PLANE,)),
            dma((PLANE,)), dma((PLANE,)),
        ],
        compiler_params=pltpu.CompilerParams(
            collective_id=0, has_side_effects=True, vmem_limit_bytes=48 * 2**20
        ),
        name="moe",
    )(tokens, norm_gain.reshape(1, width), slot_param, w_in, w_out)
    blocks = 16
    return pl.pallas_call(
        mix_kernel,
        out_shape=jax.ShapeDtypeStruct((n, width), BF16),
        in_specs=[vmem, vmem],
        out_specs=anywhere,
        scratch_shapes=[pltpu.VMEM((n, width), BF16), dma((blocks,))],
        compiler_params=pltpu.CompilerParams(vmem_limit_bytes=40 * 2**20),
        name="mix",
    )(combine, gathered)


def solution(mesh):
    in_specs = (P(("seq", "exp"), None), P(), P(), P("exp", None, "seq"), P("exp", "seq", None))
    out_specs = P(("seq", "exp"), None)
    return jax.shard_map(
        on_device, mesh=mesh, in_specs=in_specs, out_specs=out_specs, check_vma=False
    )
```

```python
import functools

import jax
import jax.numpy as jnp
from jax import lax
from jax.experimental import pallas as pl
from jax.experimental.pallas import tpu as pltpu
from jax.sharding import PartitionSpec as P

MESH = pl.DeviceIdType.MESH
F32 = jnp.float32
BF16 = jnp.bfloat16
PLANE = 16
COLUMN = 16
META = 128


def split3(v):
    hi = v.astype(BF16).astype(F32)
    rest = v - hi
    mid = rest.astype(BF16).astype(F32)
    return hi, mid, rest - mid


def meta_block(peak, total):
    rows = peak.shape[0]
    lane = lax.broadcasted_iota(jnp.int32, (rows, META), 1)
    out = jnp.zeros((rows, META), F32)
    for i, part in enumerate(split3(peak) + split3(total)):
        out = jnp.where(lane == i, part, out)
    return out.astype(BF16)


def read_meta(block):
    v = block.astype(F32)
    peak = v[:, 0:1] + v[:, 1:2] + v[:, 2:3]
    total = v[:, 3:4] + v[:, 4:5] + v[:, 5:6]
    return peak, total


def moe_kernel(
    tok, gain_hbm, slot_hbm, win_hbm, wout_hbm,
    cbuf, g_ref,
    raw, xbuf, pair, lbuf, dbuf, win, wout, gain_ref, slot_ref, mx, acc, colbuf,
    s0, r0, s1, r1, s2, r2, sl, hbuf, s4, r4,
    tsem, wsem,
    core_send, core_recv, plane_send, plane_recv, column_send, column_recv,
    back_send, back_recv, gather_send, gather_recv, fwd_send, fwd_recv,
):
    tokens, width = xbuf.shape
    slots = slot_ref.shape[1]
    half = width // 2
    group = sl.shape[1]
    piece = group // 2
    local_experts = win.shape[0]
    per = group // local_experts
    hidden = win.shape[2]
    chunks = tsem.shape[0]
    rows = tokens // chunks

    s = lax.axis_index("seq")
    e = lax.axis_index("exp")
    c = lax.rem(s, 2)
    xh = lax.rem(s // 2, 2)
    z0 = lax.rem(s // 4, 2)
    z1 = s // 8
    xl = lax.rem(e, 2)
    y0 = lax.rem(e // 2, 2)
    y1 = e // 4

    def bit(b, k, i):
        return 1 - b if (k >> i) & 1 else b

    def plane_peer(k):
        pe = (bit(y1, k, 2) * 2 + bit(y0, k, 1)) * 2 + bit(xl, k, 0)
        ph = bit(xh, k, 3)
        ps = ((z1 * 2 + z0) * 2 + ph) * 2 + c
        row = pl.multiple_of(pe * group + ph * piece, piece)
        return (ps, pe), row

    def column_peer(k):
        ph, pc = bit(xh, k, 1), bit(c, k, 0)
        ps = ((bit(z1, k, 3) * 2 + bit(z0, k, 2)) * 2 + ph) * 2 + pc
        return (ps, e), pl.multiple_of(ph * piece, piece), pc

    partner = (s + 1 - 2 * c, e)

    def remote(src, dst, send, recv, device):
        return pltpu.make_async_remote_copy(
            src_ref=src, dst_ref=dst, send_sem=send, recv_sem=recv,
            device_id=device, device_id_type=MESH,
        )

    def token_copy(i):
        at = pl.ds(pl.multiple_of(i * rows, rows), rows)
        return pltpu.make_async_copy(tok.at[at], raw.at[at], tsem.at[i])

    token_copy(0).start()
    gain_copy = pltpu.make_async_copy(gain_hbm, gain_ref, wsem.at[2])
    slot_copy = pltpu.make_async_copy(slot_hbm, slot_ref, wsem.at[3])
    gain_copy.start()
    slot_copy.start()
    for i in range(1, chunks):
        token_copy(i).start()
    barrier = pltpu.get_barrier_semaphore()
    greeted = [partner]
    greeted += [plane_peer(k)[0] for k in range(1, PLANE)]
    greeted += [column_peer(k)[0] for k in range(3, COLUMN)]
    for device in greeted:
        pl.semaphore_signal(barrier, inc=1, device_id=device, device_id_type=MESH)
    win_copy = pltpu.make_async_copy(win_hbm, win, wsem.at[0])
    wout_copy = pltpu.make_async_copy(wout_hbm, wout, wsem.at[1])

    gain_copy.wait()
    slot_copy.wait()
    gain = gain_ref[...]
    mx[...] = jnp.full(mx.shape, -jnp.inf, F32)

    def norm(i, slot):
        for q in range(rows // 32):
            at = pl.ds(pl.multiple_of(i * rows + q * 32, 32), 32)
            v = raw[at, :].astype(F32)
            scale = lax.rsqrt(jnp.mean(v * v, axis=1, keepdims=True) + 1e-06)
            normed = (v * scale * gain).astype(BF16)
            xbuf[at, :] = normed
            pair[slot][q * 32:(q + 1) * 32, :] = normed

    def project_slots(i, slot):
        at = pl.ds(pl.multiple_of(i * rows, rows), rows)
        logits = jnp.dot(pair[slot][...], slot_ref[...], preferred_element_type=F32)
        lbuf[at, :] = logits
        mx[...] = jnp.maximum(mx[...], jnp.max(logits.reshape(rows // 8, 8, slots), axis=0))

    token_copy(0).wait()
    norm(0, 0)

    @pl.loop(0, chunks // 2 - 1)
    def _(i):
        for slot in range(2):
            token_copy(2 * i + slot + 1).wait()
            norm(2 * i + slot + 1, 1 - slot)
            project_slots(2 * i + slot, slot)

    token_copy(chunks - 1).wait()
    norm(chunks - 1, 1)
    project_slots(chunks - 2, 0)
    project_slots(chunks - 1, 1)

    win_copy.start()
    wout_copy.start()
    peak = jnp.max(mx[...], axis=0, keepdims=True)

    step = min(256, tokens)

    def dispatch(i, total):
        at = pl.ds(pl.multiple_of(i * step, step), step)
        ex = jnp.exp(lbuf[at, :] - peak)
        dbuf[at, :] = ex.astype(BF16)
        return total + jnp.sum(ex.reshape(step // 8, 8, slots), axis=0)

    total = lax.fori_loop(0, tokens // step, dispatch, jnp.zeros((8, slots), F32))
    total = jnp.sum(total, axis=0, keepdims=True)
    line = lax.broadcasted_iota(jnp.int32, (META, slots), 0)
    both = jnp.where(line == 0, peak, jnp.where(line == 1, total, 0.0))
    colbuf[...] = jnp.transpose(both)
    my_meta = meta_block(colbuf[:, 0:1], colbuf[:, 1:2])

    def weigh(h):
        cols = pl.ds(pl.multiple_of(h * half, half), half)
        return lax.dot_general(
            dbuf[...], xbuf[:, cols], (((0,), (0,)), ((), ())), preferred_element_type=F32
        )

    s0[:, :half] = weigh(1 - c).astype(BF16)
    s0[:, half:] = my_meta
    pl.semaphore_wait(barrier, len(greeted))
    first_copy = remote(s0, r0, core_send.at[0], core_recv.at[0], partner)
    first_copy.start()
    acc[...] = weigh(c)
    first_copy.wait()

    mine, my_total = colbuf[:, 0:1], colbuf[:, 1:2]
    other, other_total = read_meta(r0[:, half:])
    joint = jnp.maximum(mine, other)
    wa, wb = jnp.exp(mine - joint), jnp.exp(other - joint)
    s1[:, half:] = meta_block(joint, my_total * wa + other_total * wb)
    s1[:, :half] = (acc[...] * wa + r0[:, :half].astype(F32) * wb).astype(BF16)

    order = sorted(range(1, PLANE), key=lambda k: -bin(k).count("1"))
    plane_copies = {}
    for k in order:
        device, row = plane_peer(k)
        plane_copies[k] = remote(
            s1.at[pl.ds(row, piece)], r1.at[k], plane_send.at[k], plane_recv.at[k], device
        )
        plane_copies[k].start()
    my_row = plane_peer(0)[1]

    @pl.loop(0, tokens // step, unroll=2)
    def _(i):
        at = pl.ds(pl.multiple_of(i * step, step), step)
        v = lbuf[at, :]
        ex = jnp.exp(v - jnp.max(v, axis=1, keepdims=True))
        cbuf[at, :] = (ex * (1.0 / jnp.sum(ex, axis=1, keepdims=True))).astype(BF16)

    def merge(blocks):
        metas = [read_meta(b[:, half:]) for b in blocks]
        joint = functools.reduce(jnp.maximum, [m for m, _ in metas])
        scales = [jnp.exp(m - joint) for m, _ in metas]
        out = sum(b[:, :half].astype(F32) * w for b, w in zip(blocks, scales))
        return out, joint, sum(t * w for (_, t), w in zip(metas, scales))

    for k in order:
        plane_copies[k].wait_recv()
    summed, joint, total_k = merge([s1[pl.ds(my_row, piece), :]] + [r1[k] for k in range(1, PLANE)])
    s2[:, :half] = summed.astype(BF16)
    s2[:, half:] = meta_block(joint, total_k)

    column_order = sorted(range(1, COLUMN), key=lambda k: -bin(k).count("1"))
    column_copies = {}
    for k in column_order:
        column_copies[k] = remote(
            s2, r2.at[k], column_send.at[k], column_recv.at[k], column_peer(k)[0]
        )
        column_copies[k].start()
    for k in column_order:
        column_copies[k].wait_recv()
    for low in range(4):
        blocks = [s2[...] if k == 0 else r2[k] for k in range(low, COLUMN, 4)]
        out, _, tot = merge(blocks)
        _, at, there = column_peer(low)
        sl[there, pl.ds(at, piece), :] = (out / tot).astype(BF16)
    win_copy.wait()
    wout_copy.wait()

    owner = lax.broadcasted_iota(jnp.int32, (group, hidden), 0) // per
    first = jnp.zeros((group, hidden), F32)
    for x in range(local_experts):
        y = jnp.dot(sl[0], win[x, :half, :], preferred_element_type=F32)
        y += jnp.dot(sl[1], win[x, half:, :], preferred_element_type=F32)
        first = jnp.where(owner == x, y, first)
    act = 0.5 * first * (1.0 + lax.erf(first * 0.7071067811865476))
    for x in range(local_experts):
        hbuf[:, x * hidden:(x + 1) * hidden] = jnp.where(owner == x, act, 0.0).astype(BF16)

    def project(h):
        cols = slice(h * half, (h + 1) * half)
        return sum(
            jnp.dot(hbuf[:, x * hidden:(x + 1) * hidden], wout[x, :, cols], preferred_element_type=F32)
            for x in range(local_experts)
        )

    s4[0] = project(0).astype(BF16)
    s4[1] = project(1).astype(BF16)
    back_copies = {}
    for k in column_order:
        device, at, there = column_peer(k)
        back_copies[k] = remote(
            s4.at[there, pl.ds(at, piece)], r4.at[k], back_send.at[k], back_recv.at[k], device
        )
        back_copies[k].start()
    mine = s4[c, pl.ds(column_peer(0)[1], piece), :].astype(F32)
    for k in column_order:
        back_copies[k].wait_recv()
    for k in column_order:
        mine += r4[k].astype(F32)
    at = pl.ds(my_row, piece)
    g_ref[c, at, :] = mine.astype(BF16)

    gathers = {}
    for k in order:
        gathers[k] = remote(
            g_ref.at[c, at], g_ref.at[c, at], gather_send.at[k], gather_recv.at[k], plane_peer(k)[0]
        )
        gathers[k].start()
    forwards = []
    for k in [0] + order[::-1]:
        if k:
            gathers[k].wait_recv()
        there = pl.ds(plane_peer(k)[1], piece)
        forwards.append(
            remote(g_ref.at[c, there], g_ref.at[c, there], fwd_send.at[k], fwd_recv.at[k], partner)
        )
        forwards[-1].start()
    for copy in forwards:
        copy.wait()
    for copies in (plane_copies, column_copies, back_copies, gathers):
        for copy in copies.values():
            copy.wait_send()


def mix_kernel(c_ref, g_ref, o_hbm, obuf, sem):
    half = g_ref.shape[2]
    blocks = sem.shape[0]
    rows = obuf.shape[0] // blocks
    copies = []
    for i in range(blocks):
        at = pl.ds(i * rows, rows)
        for h in range(2):
            obuf[at, h * half:(h + 1) * half] = jnp.dot(
                c_ref[at, :], g_ref[h], preferred_element_type=F32
            ).astype(BF16)
        copies.append(pltpu.make_async_copy(obuf.at[at], o_hbm.at[at], sem.at[i]))
        copies[-1].start()
    for copy in copies:
        copy.wait()


def on_device(tokens, norm_gain, slot_param, w_in, w_out):
    n, width = tokens.shape
    slots = slot_param.shape[1]
    half = width // 2
    group = slots // lax.axis_size("exp")
    piece = group // 2
    hidden = w_in.shape[2]
    chunks = 8
    wide = half + META
    dma = pltpu.SemaphoreType.DMA
    anywhere = pl.BlockSpec(memory_space=pltpu.HBM)
    vmem = pl.BlockSpec(memory_space=pltpu.VMEM)
    combine, gathered = pl.pallas_call(
        moe_kernel,
        out_shape=(
            pltpu.VMEM((n, slots), BF16),
            pltpu.VMEM((2, slots, half), BF16),
        ),
        in_specs=[anywhere] * 5,
        out_specs=(vmem, vmem),
        scratch_shapes=[
            pltpu.VMEM((n, width), BF16),
            pltpu.VMEM((n, width), BF16),
            [pltpu.VMEM((n // chunks, width), BF16)] * 2,
            pltpu.VMEM((n, slots), F32),
            pltpu.VMEM((n, slots), BF16),
            pltpu.VMEM(w_in.shape, BF16),
            pltpu.VMEM(w_out.shape, BF16),
            pltpu.VMEM((1, width), F32),
            pltpu.VMEM((width, slots), BF16),
            pltpu.VMEM((8, slots), F32),
            pltpu.VMEM((slots, half), F32),
            pltpu.VMEM((slots, META), F32),
            pltpu.VMEM((slots, wide), BF16),
            pltpu.VMEM((slots, wide), BF16),
            pltpu.VMEM((slots, wide), BF16),
            pltpu.VMEM((PLANE, piece, wide), BF16),
            pltpu.VMEM((piece, wide), BF16),
            pltpu.VMEM((COLUMN, piece, wide), BF16),
            pltpu.VMEM((2, group, half), BF16),
            pltpu.VMEM((group, w_in.shape[0] * hidden), BF16),
            pltpu.VMEM((2, group, half), BF16),
            pltpu.VMEM((COLUMN, piece, half), BF16),
            dma((chunks,)),
            dma((4,)),
            dma((1,)), dma((1,)),
            dma((PLANE,)), dma((PLANE,)),
            dma((COLUMN,)), dma((COLUMN,)),
            dma((COLUMN,)), dma((COLUMN,)),
            dma((PLANE,)), dma((PLANE,)),
            dma((PLANE,)), dma((PLANE,)),
        ],
        compiler_params=pltpu.CompilerParams(
            collective_id=0, has_side_effects=True, vmem_limit_bytes=48 * 2**20
        ),
        name="moe",
    )(
        *(
            pltpu.with_memory_space_constraint(a, pltpu.HBM)
            for a in (tokens, norm_gain.reshape(1, width), slot_param, w_in, w_out)
        )
    )
    blocks = 16
    return pl.pallas_call(
        mix_kernel,
        out_shape=jax.ShapeDtypeStruct((n, width), BF16),
        in_specs=[vmem, vmem],
        out_specs=anywhere,
        scratch_shapes=[pltpu.VMEM((n, width), BF16), dma((blocks,))],
        compiler_params=pltpu.CompilerParams(vmem_limit_bytes=40 * 2**20),
        name="mix",
    )(combine, gathered)


def solution(mesh):
    in_specs = (P(("seq", "exp"), None), P(), P(), P("exp", None, "seq"), P("exp", "seq", None))
    out_specs = P(("seq", "exp"), None)
    return jax.shard_map(
        on_device, mesh=mesh, in_specs=in_specs, out_specs=out_specs, check_vma=False
    )
```

```python
import functools

import jax
import jax.numpy as jnp
from jax import lax
from jax.experimental import pallas as pl
from jax.experimental.pallas import tpu as pltpu
from jax.sharding import PartitionSpec as P

MESH = pl.DeviceIdType.MESH
F32 = jnp.float32
BF16 = jnp.bfloat16
PLANE = 16
COLUMN = 8
META = 128


def split3(v):
    hi = v.astype(BF16).astype(F32)
    rest = v - hi
    mid = rest.astype(BF16).astype(F32)
    return hi, mid, rest - mid


def meta_block(peak, total):
    rows = peak.shape[0]
    lane = lax.broadcasted_iota(jnp.int32, (rows, META), 1)
    out = jnp.zeros((rows, META), F32)
    for i, part in enumerate(split3(peak) + split3(total)):
        out = jnp.where(lane == i, part, out)
    return out.astype(BF16)


def read_meta(block):
    v = block.astype(F32)
    peak = v[:, 0:1] + v[:, 1:2] + v[:, 2:3]
    total = v[:, 3:4] + v[:, 4:5] + v[:, 5:6]
    return peak, total


def moe_kernel(
    tok, gain_hbm, slot_hbm, win_hbm, wout_hbm,
    cbuf, g_ref, begun,
    raw, xbuf, pair, lbuf, dbuf, win, wout, gain_ref, slot_ref, mx, acc, colbuf,
    s0, r0, s1, r1, s2, r2, sl, hbuf, xs, xr, s4, r4,
    tsem, wsem,
    core_send, core_recv, plane_send, plane_recv, column_send, column_recv,
    back_send, back_recv, gather_send, gather_recv, fwd_send, fwd_recv,
):
    tokens, width = xbuf.shape
    slots = slot_ref.shape[1]
    half = width // 2
    group = sl.shape[1]
    piece = group // 2
    local_experts = win.shape[0]
    per = group // local_experts
    hidden = win.shape[2]
    chunks = tsem.shape[0]
    rows = tokens // chunks

    s = lax.axis_index("seq")
    e = lax.axis_index("exp")
    c = lax.rem(s, 2)
    xh = lax.rem(s // 2, 2)
    z0 = lax.rem(s // 4, 2)
    z1 = s // 8
    xl = lax.rem(e, 2)
    y0 = lax.rem(e // 2, 2)
    y1 = e // 4

    def bit(b, k, i):
        return 1 - b if (k >> i) & 1 else b

    def plane_peer(k):
        pe = (bit(y1, k, 2) * 2 + bit(y0, k, 1)) * 2 + bit(xl, k, 0)
        ph = bit(xh, k, 3)
        ps = ((z1 * 2 + z0) * 2 + ph) * 2 + c
        row = pl.multiple_of(pe * group + ph * piece, piece)
        return (ps, pe), row

    def column_peer(k):
        ph = bit(xh, k, 0)
        ps = ((bit(z1, k, 2) * 2 + bit(z0, k, 1)) * 2 + ph) * 2 + c
        return (ps, e), pl.multiple_of(ph * piece, piece)

    partner = (s + 1 - 2 * c, e)

    def remote(src, dst, send, recv, device):
        return pltpu.make_async_remote_copy(
            src_ref=src, dst_ref=dst, send_sem=send, recv_sem=recv,
            device_id=device, device_id_type=MESH,
        )

    def token_copy(i):
        at = pl.ds(pl.multiple_of(i * rows, rows), rows)
        return pltpu.make_async_copy(tok.at[at], raw.at[at], tsem.at[i])

    token_copy(0).start()
    gain_copy = pltpu.make_async_copy(gain_hbm, gain_ref, wsem.at[2])
    slot_copy = pltpu.make_async_copy(slot_hbm, slot_ref, wsem.at[3])
    gain_copy.start()
    slot_copy.start()
    for i in range(1, chunks):
        token_copy(i).start()
    barrier = pltpu.get_barrier_semaphore()
    greeted = [partner]
    greeted += [plane_peer(k)[0] for k in range(1, PLANE)]
    greeted += [column_peer(k)[0] for k in range(2, COLUMN)]
    for device in greeted:
        pl.semaphore_signal(barrier, inc=1, device_id=device, device_id_type=MESH)
    win_copy = pltpu.make_async_copy(win_hbm, win, wsem.at[0])
    wout_copy = pltpu.make_async_copy(wout_hbm, wout, wsem.at[1])

    gain_copy.wait()
    slot_copy.wait()
    gain = gain_ref[...]
    mx[...] = jnp.full(mx.shape, -jnp.inf, F32)

    def norm(i, slot):
        for q in range(rows // 32):
            at = pl.ds(pl.multiple_of(i * rows + q * 32, 32), 32)
            v = raw[at, :].astype(F32)
            scale = lax.rsqrt(jnp.mean(v * v, axis=1, keepdims=True) + 1e-06)
            normed = (v * scale * gain).astype(BF16)
            xbuf[at, :] = normed
            pair[slot][q * 32:(q + 1) * 32, :] = normed

    def project_slots(i, slot):
        at = pl.ds(pl.multiple_of(i * rows, rows), rows)
        logits = jnp.dot(pair[slot][...], slot_ref[...], preferred_element_type=F32)
        lbuf[at, :] = logits
        mx[...] = jnp.maximum(mx[...], jnp.max(logits.reshape(rows // 8, 8, slots), axis=0))

    token_copy(0).wait()
    norm(0, 0)

    @pl.loop(0, chunks // 2 - 1)
    def _(i):
        for slot in range(2):
            token_copy(2 * i + slot + 1).wait()
            norm(2 * i + slot + 1, 1 - slot)
            project_slots(2 * i + slot, slot)

    token_copy(chunks - 1).wait()
    norm(chunks - 1, 1)
    project_slots(chunks - 2, 0)
    project_slots(chunks - 1, 1)

    win_copy.start()
    wout_copy.start()
    peak = jnp.max(mx[...], axis=0, keepdims=True)

    step = min(256, tokens)

    def dispatch(i, total):
        at = pl.ds(pl.multiple_of(i * step, step), step)
        ex = jnp.exp(lbuf[at, :] - peak)
        dbuf[at, :] = ex.astype(BF16)
        return total + jnp.sum(ex.reshape(step // 8, 8, slots), axis=0)

    total = lax.fori_loop(0, tokens // step, dispatch, jnp.zeros((8, slots), F32))
    total = jnp.sum(total, axis=0, keepdims=True)
    line = lax.broadcasted_iota(jnp.int32, (META, slots), 0)
    both = jnp.where(line == 0, peak, jnp.where(line == 1, total, 0.0))
    colbuf[...] = jnp.transpose(both)
    my_meta = meta_block(colbuf[:, 0:1], colbuf[:, 1:2])

    def weigh(h):
        cols = pl.ds(pl.multiple_of(h * half, half), half)
        return lax.dot_general(
            dbuf[...], xbuf[:, cols], (((0,), (0,)), ((), ())), preferred_element_type=F32
        )

    s0[:, :half] = weigh(1 - c).astype(BF16)
    s0[:, half:] = my_meta
    pl.semaphore_wait(barrier, len(greeted))
    first_copy = remote(s0, r0, core_send.at[0], core_recv.at[0], partner)
    first_copy.start()
    acc[...] = weigh(c)
    first_copy.wait()

    mine, my_total = colbuf[:, 0:1], colbuf[:, 1:2]
    other, other_total = read_meta(r0[:, half:])
    joint = jnp.maximum(mine, other)
    wa, wb = jnp.exp(mine - joint), jnp.exp(other - joint)
    s1[:, half:] = meta_block(joint, my_total * wa + other_total * wb)
    s1[:, :half] = (acc[...] * wa + r0[:, :half].astype(F32) * wb).astype(BF16)

    order = sorted(range(1, PLANE), key=lambda k: -bin(k).count("1"))
    plane_copies = {}
    for k in order:
        device, row = plane_peer(k)
        plane_copies[k] = remote(
            s1.at[pl.ds(row, piece)], r1.at[k], plane_send.at[k], plane_recv.at[k], device
        )
        plane_copies[k].start()
    my_row = plane_peer(0)[1]

    @pl.loop(0, tokens // step, unroll=2)
    def _(i):
        at = pl.ds(pl.multiple_of(i * step, step), step)
        v = lbuf[at, :]
        ex = jnp.exp(v - jnp.max(v, axis=1, keepdims=True))
        cbuf[at, :] = (ex * (1.0 / jnp.sum(ex, axis=1, keepdims=True))).astype(BF16)

    def merge(blocks):
        metas = [read_meta(b[:, half:]) for b in blocks]
        joint = functools.reduce(jnp.maximum, [m for m, _ in metas])
        scales = [jnp.exp(m - joint) for m, _ in metas]
        out = sum(b[:, :half].astype(F32) * w for b, w in zip(blocks, scales))
        return out, joint, sum(t * w for (_, t), w in zip(metas, scales))

    for k in order:
        plane_copies[k].wait_recv()
    summed, joint, total_k = merge([s1[pl.ds(my_row, piece), :]] + [r1[k] for k in range(1, PLANE)])
    s2[:, :half] = summed.astype(BF16)
    s2[:, half:] = meta_block(joint, total_k)

    column_order = sorted(range(1, COLUMN), key=lambda k: -bin(k).count("1"))
    column_copies = {}
    for k in column_order:
        column_copies[k] = remote(
            s2, r2.at[k], column_send.at[k], column_recv.at[k], column_peer(k)[0]
        )
        column_copies[k].start()
    for k in column_order:
        column_copies[k].wait_recv()
    for low in range(2):
        out, _, tot = merge([s2[...] if k == 0 else r2[k] for k in range(low, COLUMN, 2)])
        sl[c, pl.ds(column_peer(low)[1], piece), :] = (out / tot).astype(BF16)
    in_copy = remote(sl.at[c], sl.at[c], core_send.at[1], core_recv.at[1], partner)
    in_copy.start()
    win_copy.wait()
    wout_copy.wait()

    owner = lax.broadcasted_iota(jnp.int32, (group, hidden), 0) // per

    def enter(h, first):
        rows_in = pl.ds(pl.multiple_of(h * half, half), half)
        for x in range(local_experts):
            y = jnp.dot(sl[h], win[x, rows_in, :], preferred_element_type=F32)
            first = jnp.where(owner == x, first + y, first)
        return first

    first = enter(c, jnp.zeros((group, hidden), F32))
    in_copy.wait()
    first = enter(1 - c, first)
    act = 0.5 * first * (1.0 + lax.erf(first * 0.7071067811865476))
    for x in range(local_experts):
        hbuf[:, x * hidden:(x + 1) * hidden] = jnp.where(owner == x, act, 0.0).astype(BF16)

    def project(h):
        cols = pl.ds(pl.multiple_of(h * half, half), half)
        return sum(
            jnp.dot(hbuf[:, x * hidden:(x + 1) * hidden], wout[x, :, cols], preferred_element_type=F32)
            for x in range(local_experts)
        )

    xs[...] = project(1 - c).astype(BF16)
    out_copy = remote(xs, xr, core_send.at[2], core_recv.at[2], partner)
    out_copy.start()
    own = project(c)
    out_copy.wait()
    s4[...] = (own + xr[...].astype(F32)).astype(BF16)
    back_copies = {}
    for k in column_order:
        device, at = column_peer(k)
        back_copies[k] = remote(
            s4.at[pl.ds(at, piece)], r4.at[k], back_send.at[k], back_recv.at[k], device
        )
        back_copies[k].start()
    mine = s4[pl.ds(column_peer(0)[1], piece), :].astype(F32)
    for k in column_order:
        back_copies[k].wait_recv()
    for k in column_order:
        mine += r4[k].astype(F32)
    at = pl.ds(my_row, piece)
    g_ref[c, at, :] = mine.astype(BF16)

    gathers = {}
    for k in order:
        gathers[k] = remote(
            g_ref.at[c, at], g_ref.at[c, at], gather_send.at[k], gather_recv.at[k], plane_peer(k)[0]
        )
        gathers[k].start()
    forwards = []
    for k in [0] + order[::-1]:
        if k:
            gathers[k].wait_recv()
        there = pl.ds(plane_peer(k)[1], piece)
        forwards.append(
            remote(g_ref.at[c, there], g_ref.at[c, there], fwd_send.at[k], fwd_recv.at[k], partner)
        )
        forwards[-1].start()
    for i in range(4):
        at = pl.ds(i * (tokens // 4), tokens // 4)
        begun[at, :] = jnp.dot(
            cbuf[at, :], g_ref[c], preferred_element_type=F32
        ).astype(BF16)
    for copy in forwards:
        copy.wait()
    for copies in (plane_copies, column_copies, back_copies, gathers):
        for copy in copies.values():
            copy.wait_send()


def mix_kernel(c_ref, g_ref, begun, o_hbm, obuf, sem, begun_sem):
    half = g_ref.shape[2]
    blocks = sem.shape[0]
    rows = obuf.shape[0] // blocks
    c = lax.rem(lax.axis_index("seq"), 2)
    mine = pl.ds(pl.multiple_of(c * half, half), half)
    rest = pl.ds(pl.multiple_of((1 - c) * half, half), half)
    copies = [pltpu.make_async_copy(begun, o_hbm.at[:, mine], begun_sem.at[0])]
    copies[0].start()
    for i in range(blocks):
        at = pl.ds(i * rows, rows)
        obuf[at, :] = jnp.dot(
            c_ref[at, :], g_ref[1 - c], preferred_element_type=F32
        ).astype(BF16)
        copies.append(pltpu.make_async_copy(obuf.at[at], o_hbm.at[at, rest], sem.at[i]))
        copies[-1].start()
    for copy in copies:
        copy.wait()


def on_device(tokens, norm_gain, slot_param, w_in, w_out):
    n, width = tokens.shape
    slots = slot_param.shape[1]
    half = width // 2
    group = slots // lax.axis_size("exp")
    piece = group // 2
    hidden = w_in.shape[2]
    chunks = 8
    wide = half + META
    dma = pltpu.SemaphoreType.DMA
    anywhere = pl.BlockSpec(memory_space=pltpu.HBM)
    vmem = pl.BlockSpec(memory_space=pltpu.VMEM)
    combine, gathered, begun = pl.pallas_call(
        moe_kernel,
        out_shape=(
            pltpu.VMEM((n, slots), BF16),
            pltpu.VMEM((2, slots, half), BF16),
            pltpu.VMEM((n, half), BF16),
        ),
        in_specs=[anywhere] * 5,
        out_specs=(vmem, vmem, vmem),
        scratch_shapes=[
            pltpu.VMEM((n, width), BF16),
            pltpu.VMEM((n, width), BF16),
            [pltpu.VMEM((n // chunks, width), BF16)] * 2,
            pltpu.VMEM((n, slots), F32),
            pltpu.VMEM((n, slots), BF16),
            pltpu.VMEM(w_in.shape, BF16),
            pltpu.VMEM(w_out.shape, BF16),
            pltpu.VMEM((1, width), F32),
            pltpu.VMEM((width, slots), BF16),
            pltpu.VMEM((8, slots), F32),
            pltpu.VMEM((slots, half), F32),
            pltpu.VMEM((slots, META), F32),
            pltpu.VMEM((slots, wide), BF16),
            pltpu.VMEM((slots, wide), BF16),
            pltpu.VMEM((slots, wide), BF16),
            pltpu.VMEM((PLANE, piece, wide), BF16),
            pltpu.VMEM((piece, wide), BF16),
            pltpu.VMEM((COLUMN, piece, wide), BF16),
            pltpu.VMEM((2, group, half), BF16),
            pltpu.VMEM((group, w_in.shape[0] * hidden), BF16),
            pltpu.VMEM((group, half), BF16),
            pltpu.VMEM((group, half), BF16),
            pltpu.VMEM((group, half), BF16),
            pltpu.VMEM((COLUMN, piece, half), BF16),
            dma((chunks,)),
            dma((4,)),
            dma((3,)), dma((3,)),
            dma((PLANE,)), dma((PLANE,)),
            dma((COLUMN,)), dma((COLUMN,)),
            dma((COLUMN,)), dma((COLUMN,)),
            dma((PLANE,)), dma((PLANE,)),
            dma((PLANE,)), dma((PLANE,)),
        ],
        compiler_params=pltpu.CompilerParams(
            collective_id=0, has_side_effects=True, vmem_limit_bytes=48 * 2**20
        ),
        name="moe",
    )(
        *(
            pltpu.with_memory_space_constraint(a, pltpu.HBM)
            for a in (tokens, norm_gain.reshape(1, width), slot_param, w_in, w_out)
        )
    )
    return pl.pallas_call(
        mix_kernel,
        out_shape=jax.ShapeDtypeStruct((n, width), BF16),
        in_specs=[vmem, vmem, vmem],
        out_specs=anywhere,
        scratch_shapes=[pltpu.VMEM((n, half), BF16), dma((8,)), dma((1,))],
        compiler_params=pltpu.CompilerParams(vmem_limit_bytes=40 * 2**20),
        name="mix",
    )(combine, gathered, begun)


def solution(mesh):
    in_specs = (P(("seq", "exp"), None), P(), P(), P("exp", None, "seq"), P("exp", "seq", None))
    out_specs = P(("seq", "exp"), None)
    return jax.shard_map(
        on_device, mesh=mesh, in_specs=in_specs, out_specs=out_specs, check_vma=False
    )
```

```python
import functools

import jax
import jax.numpy as jnp
from jax import lax
from jax.experimental import pallas as pl
from jax.experimental.pallas import tpu as pltpu
from jax.sharding import PartitionSpec as P

MESH = pl.DeviceIdType.MESH
F32 = jnp.float32
BF16 = jnp.bfloat16
PLANE = 16
COLUMN = 8
META = 128


def split3(v):
    hi = v.astype(BF16).astype(F32)
    rest = v - hi
    mid = rest.astype(BF16).astype(F32)
    return hi, mid, rest - mid


def meta_block(peak, total):
    rows = peak.shape[0]
    lane = lax.broadcasted_iota(jnp.int32, (rows, META), 1)
    out = jnp.zeros((rows, META), F32)
    for i, part in enumerate(split3(peak) + split3(total)):
        out = jnp.where(lane == i, part, out)
    return out.astype(BF16)


def read_meta(block):
    v = block.astype(F32)
    peak = v[:, 0:1] + v[:, 1:2] + v[:, 2:3]
    total = v[:, 3:4] + v[:, 4:5] + v[:, 5:6]
    return peak, total


def moe_kernel(
    tok, gain_hbm, slot_hbm, win_hbm, wout_hbm,
    cbuf, g_ref, begun,
    raw, xbuf, pair, lbuf, dbuf, win, wout, gain_ref, slot_ref, mx, acc, colbuf,
    s0, r0, s1, r1, s2, r2, sl, hbuf, xs, xr, s4, r4,
    tsem, wsem,
    core_send, core_recv, plane_send, plane_recv, column_send, column_recv,
    back_send, back_recv, gather_send, gather_recv, fwd_send, fwd_recv,
):
    tokens, width = xbuf.shape
    slots = slot_ref.shape[1]
    half = width // 2
    group = sl.shape[1]
    piece = group // 2
    local_experts = win.shape[0]
    per = group // local_experts
    hidden = win.shape[2]
    chunks = tsem.shape[0]
    rows = tokens // chunks

    s = lax.axis_index("seq")
    e = lax.axis_index("exp")
    c = lax.rem(s, 2)
    xh = lax.rem(s // 2, 2)
    z0 = lax.rem(s // 4, 2)
    z1 = s // 8
    xl = lax.rem(e, 2)
    y0 = lax.rem(e // 2, 2)
    y1 = e // 4

    def bit(b, k, i):
        return 1 - b if (k >> i) & 1 else b

    def plane_peer(k):
        pe = (bit(y1, k, 2) * 2 + bit(y0, k, 1)) * 2 + bit(xl, k, 0)
        ph = bit(xh, k, 3)
        ps = ((z1 * 2 + z0) * 2 + ph) * 2 + c
        row = pl.multiple_of(pe * group + ph * piece, piece)
        return (ps, pe), row

    def column_peer(k):
        ph = bit(xh, k, 0)
        ps = ((bit(z1, k, 2) * 2 + bit(z0, k, 1)) * 2 + ph) * 2 + c
        return (ps, e), pl.multiple_of(ph * piece, piece)

    partner = (s + 1 - 2 * c, e)

    def remote(src, dst, send, recv, device):
        return pltpu.make_async_remote_copy(
            src_ref=src, dst_ref=dst, send_sem=send, recv_sem=recv,
            device_id=device, device_id_type=MESH,
        )

    def token_copy(i):
        at = pl.ds(pl.multiple_of(i * rows, rows), rows)
        return pltpu.make_async_copy(tok.at[at], raw.at[at], tsem.at[i])

    gain_copy = pltpu.make_async_copy(gain_hbm, gain_ref, wsem.at[2])
    slot_copy = pltpu.make_async_copy(slot_hbm, slot_ref, wsem.at[3])
    gain_copy.start()
    token_copy(0).start()
    slot_copy.start()
    for i in range(1, chunks):
        token_copy(i).start()
    barrier = pltpu.get_barrier_semaphore()
    greeted = [partner]
    greeted += [plane_peer(k)[0] for k in range(1, PLANE)]
    greeted += [column_peer(k)[0] for k in range(2, COLUMN)]
    for device in greeted:
        pl.semaphore_signal(barrier, inc=1, device_id=device, device_id_type=MESH)
    win_copy = pltpu.make_async_copy(win_hbm, win, wsem.at[0])
    wout_copy = pltpu.make_async_copy(wout_hbm, wout, wsem.at[1])

    gain_copy.wait()
    gain = gain_ref[...]
    mx[...] = jnp.full(mx.shape, -jnp.inf, F32)

    def norm(i, slot):
        for q in range(rows // 32):
            at = pl.ds(pl.multiple_of(i * rows + q * 32, 32), 32)
            v = raw[at, :].astype(F32)
            scale = lax.rsqrt(jnp.mean(v * v, axis=1, keepdims=True) + 1e-06)
            normed = (v * scale * gain).astype(BF16)
            xbuf[at, :] = normed
            pair[slot][q * 32:(q + 1) * 32, :] = normed

    def project_slots(i, slot):
        at = pl.ds(pl.multiple_of(i * rows, rows), rows)
        logits = jnp.dot(pair[slot][...], slot_ref[...], preferred_element_type=F32)
        lbuf[at, :] = logits
        mx[...] = jnp.maximum(mx[...], jnp.max(logits.reshape(rows // 8, 8, slots), axis=0))

    token_copy(0).wait()
    norm(0, 0)
    slot_copy.wait()

    @pl.loop(0, chunks // 2 - 1)
    def _(i):
        token_copy(2 * i + 1).wait()
        token_copy(2 * i + 2).wait()
        for slot in range(2):
            norm(2 * i + slot + 1, 1 - slot)
            project_slots(2 * i + slot, slot)

    token_copy(chunks - 1).wait()
    norm(chunks - 1, 1)
    project_slots(chunks - 2, 0)
    project_slots(chunks - 1, 1)

    win_copy.start()
    wout_copy.start()
    peak = jnp.max(mx[...], axis=0, keepdims=True)

    step = min(256, tokens)

    def dispatch(i, total):
        at = pl.ds(pl.multiple_of(i * step, step), step)
        ex = jnp.exp(lbuf[at, :] - peak)
        dbuf[at, :] = ex.astype(BF16)
        return total + jnp.sum(ex.reshape(step // 8, 8, slots), axis=0)

    total = lax.fori_loop(0, tokens // step, dispatch, jnp.zeros((8, slots), F32))
    total = jnp.sum(total, axis=0, keepdims=True)
    line = lax.broadcasted_iota(jnp.int32, (META, slots), 0)
    both = jnp.where(line == 0, peak, jnp.where(line == 1, total, 0.0))
    colbuf[...] = jnp.transpose(both)
    my_meta = meta_block(colbuf[:, 0:1], colbuf[:, 1:2])

    def weigh(h):
        cols = pl.ds(pl.multiple_of(h * half, half), half)
        return lax.dot_general(
            dbuf[...], xbuf[:, cols], (((0,), (0,)), ((), ())), preferred_element_type=F32
        )

    s0[:, :half] = weigh(1 - c).astype(BF16)
    s0[:, half:] = my_meta
    pl.semaphore_wait(barrier, len(greeted))
    first_copy = remote(s0, r0, core_send.at[0], core_recv.at[0], partner)
    first_copy.start()
    acc[...] = weigh(c)
    first_copy.wait()

    mine, my_total = colbuf[:, 0:1], colbuf[:, 1:2]
    other, other_total = read_meta(r0[:, half:])
    joint = jnp.maximum(mine, other)
    wa, wb = jnp.exp(mine - joint), jnp.exp(other - joint)
    s1[:, half:] = meta_block(joint, my_total * wa + other_total * wb)
    s1[:, :half] = (acc[...] * wa + r0[:, :half].astype(F32) * wb).astype(BF16)

    order = sorted(range(1, PLANE), key=lambda k: -bin(k).count("1"))
    plane_copies = {}
    for k in order:
        device, row = plane_peer(k)
        plane_copies[k] = remote(
            s1.at[pl.ds(row, piece)], r1.at[k], plane_send.at[k], plane_recv.at[k], device
        )
        plane_copies[k].start()
    my_row = plane_peer(0)[1]

    @pl.loop(0, tokens // step, unroll=2)
    def _(i):
        at = pl.ds(pl.multiple_of(i * step, step), step)
        v = lbuf[at, :]
        ex = jnp.exp(v - jnp.max(v, axis=1, keepdims=True))
        cbuf[at, :] = (ex * (1.0 / jnp.sum(ex, axis=1, keepdims=True))).astype(BF16)

    def merge(blocks):
        metas = [read_meta(b[:, half:]) for b in blocks]
        joint = functools.reduce(jnp.maximum, [m for m, _ in metas])
        scales = [jnp.exp(m - joint) for m, _ in metas]
        out = sum(b[:, :half].astype(F32) * w for b, w in zip(blocks, scales))
        return out, joint, sum(t * w for (_, t), w in zip(metas, scales))

    for k in order:
        plane_copies[k].wait_recv()
    summed, joint, total_k = merge([s1[pl.ds(my_row, piece), :]] + [r1[k] for k in range(1, PLANE)])
    s2[:, :half] = summed.astype(BF16)
    s2[:, half:] = meta_block(joint, total_k)

    column_order = sorted(range(1, COLUMN), key=lambda k: -bin(k).count("1"))
    column_copies = {}
    for k in column_order:
        column_copies[k] = remote(
            s2, r2.at[k], column_send.at[k], column_recv.at[k], column_peer(k)[0]
        )
        column_copies[k].start()
    for k in column_order:
        column_copies[k].wait_recv()
    for low in range(2):
        out, _, tot = merge([s2[...] if k == 0 else r2[k] for k in range(low, COLUMN, 2)])
        sl[c, pl.ds(column_peer(low)[1], piece), :] = (out / tot).astype(BF16)
    in_copy = remote(sl.at[c], sl.at[c], core_send.at[1], core_recv.at[1], partner)
    in_copy.start()
    win_copy.wait()
    wout_copy.wait()

    owner = lax.broadcasted_iota(jnp.int32, (group, hidden), 0) // per

    def enter(h, first):
        rows_in = pl.ds(pl.multiple_of(h * half, half), half)
        for x in range(local_experts):
            y = jnp.dot(sl[h], win[x, rows_in, :], preferred_element_type=F32)
            first = jnp.where(owner == x, first + y, first)
        return first

    first = enter(c, jnp.zeros((group, hidden), F32))
    in_copy.wait()
    first = enter(1 - c, first)
    act = 0.5 * first * (1.0 + lax.erf(first * 0.7071067811865476))
    for x in range(local_experts):
        hbuf[:, x * hidden:(x + 1) * hidden] = jnp.where(owner == x, act, 0.0).astype(BF16)

    def project(h):
        cols = pl.ds(pl.multiple_of(h * half, half), half)
        return sum(
            jnp.dot(hbuf[:, x * hidden:(x + 1) * hidden], wout[x, :, cols], preferred_element_type=F32)
            for x in range(local_experts)
        )

    xs[...] = project(1 - c).astype(BF16)
    out_copy = remote(xs, xr, core_send.at[2], core_recv.at[2], partner)
    out_copy.start()
    own = project(c)
    out_copy.wait()
    s4[...] = (own + xr[...].astype(F32)).astype(BF16)
    back_copies = {}
    for k in column_order:
        device, at = column_peer(k)
        back_copies[k] = remote(
            s4.at[pl.ds(at, piece)], r4.at[k], back_send.at[k], back_recv.at[k], device
        )
        back_copies[k].start()
    mine = s4[pl.ds(column_peer(0)[1], piece), :].astype(F32)
    for k in column_order:
        back_copies[k].wait_recv()
    for k in column_order:
        mine += r4[k].astype(F32)
    at = pl.ds(my_row, piece)
    g_ref[c, at, :] = mine.astype(BF16)

    gathers = {}
    for k in order:
        gathers[k] = remote(
            g_ref.at[c, at], g_ref.at[c, at], gather_send.at[k], gather_recv.at[k], plane_peer(k)[0]
        )
        gathers[k].start()
    forwards = []
    for k in [0] + order[::-1]:
        if k:
            gathers[k].wait_recv()
        there = pl.ds(plane_peer(k)[1], piece)
        forwards.append(
            remote(g_ref.at[c, there], g_ref.at[c, there], fwd_send.at[k], fwd_recv.at[k], partner)
        )
        forwards[-1].start()
    early = begun.shape[0] // 2
    for i in range(2):
        at = pl.ds(i * early, early)
        begun[at, :] = jnp.dot(
            cbuf[at, :], g_ref[c], preferred_element_type=F32
        ).astype(BF16)
    for copy in forwards:
        copy.wait()
    for copies in (plane_copies, column_copies, back_copies, gathers):
        for copy in copies.values():
            copy.wait_send()


def mix_kernel(c_ref, g_ref, begun, o_hbm, obuf, sem, begun_sem):
    half = g_ref.shape[2]
    rows = obuf.shape[1]
    blocks = o_hbm.shape[0] // rows
    c = lax.rem(lax.axis_index("seq"), 2)
    mine = pl.ds(pl.multiple_of(c * half, half), half)
    rest = pl.ds(pl.multiple_of((1 - c) * half, half), half)
    early = begun.shape[0]
    copies = [pltpu.make_async_copy(begun, o_hbm.at[pl.ds(0, early), mine], begun_sem.at[0])]
    copies[0].start()
    todo = [(i * rows, 1 - c, rest) for i in range(blocks)]
    todo += [(i * rows, c, mine) for i in range(early // rows, blocks)]
    for i, (row, h, cols) in enumerate(todo):
        at = pl.ds(row, rows)
        obuf[i] = jnp.dot(c_ref[at, :], g_ref[h], preferred_element_type=F32).astype(BF16)
        copies.append(pltpu.make_async_copy(obuf.at[i], o_hbm.at[at, cols], sem.at[i]))
        copies[-1].start()
    for copy in copies:
        copy.wait()


def on_device(tokens, norm_gain, slot_param, w_in, w_out):
    n, width = tokens.shape
    slots = slot_param.shape[1]
    half = width // 2
    group = slots // lax.axis_size("exp")
    piece = group // 2
    hidden = w_in.shape[2]
    chunks = 16
    wide = half + META
    dma = pltpu.SemaphoreType.DMA
    anywhere = pl.BlockSpec(memory_space=pltpu.HBM)
    vmem = pl.BlockSpec(memory_space=pltpu.VMEM)
    combine, gathered, begun = pl.pallas_call(
        moe_kernel,
        out_shape=(
            pltpu.VMEM((n, slots), BF16),
            pltpu.VMEM((2, slots, half), BF16),
            pltpu.VMEM((n // 2, half), BF16),
        ),
        in_specs=[anywhere] * 5,
        out_specs=(vmem, vmem, vmem),
        scratch_shapes=[
            pltpu.VMEM((n, width), BF16),
            pltpu.VMEM((n, width), BF16),
            [pltpu.VMEM((n // chunks, width), BF16)] * 2,
            pltpu.VMEM((n, slots), F32),
            pltpu.VMEM((n, slots), BF16),
            pltpu.VMEM(w_in.shape, BF16),
            pltpu.VMEM(w_out.shape, BF16),
            pltpu.VMEM((1, width), F32),
            pltpu.VMEM((width, slots), BF16),
            pltpu.VMEM((8, slots), F32),
            pltpu.VMEM((slots, half), F32),
            pltpu.VMEM((slots, META), F32),
            pltpu.VMEM((slots, wide), BF16),
            pltpu.VMEM((slots, wide), BF16),
            pltpu.VMEM((slots, wide), BF16),
            pltpu.VMEM((PLANE, piece, wide), BF16),
            pltpu.VMEM((piece, wide), BF16),
            pltpu.VMEM((COLUMN, piece, wide), BF16),
            pltpu.VMEM((2, group, half), BF16),
            pltpu.VMEM((group, w_in.shape[0] * hidden), BF16),
            pltpu.VMEM((group, half), BF16),
            pltpu.VMEM((group, half), BF16),
            pltpu.VMEM((group, half), BF16),
            pltpu.VMEM((COLUMN, piece, half), BF16),
            dma((chunks,)),
            dma((4,)),
            dma((3,)), dma((3,)),
            dma((PLANE,)), dma((PLANE,)),
            dma((COLUMN,)), dma((COLUMN,)),
            dma((COLUMN,)), dma((COLUMN,)),
            dma((PLANE,)), dma((PLANE,)),
            dma((PLANE,)), dma((PLANE,)),
        ],
        compiler_params=pltpu.CompilerParams(
            collective_id=0, has_side_effects=True, vmem_limit_bytes=48 * 2**20
        ),
        name="moe",
    )(
        *(
            pltpu.with_memory_space_constraint(a, pltpu.HBM)
            for a in (tokens, norm_gain.reshape(1, width), slot_param, w_in, w_out)
        )
    )
    return pl.pallas_call(
        mix_kernel,
        out_shape=jax.ShapeDtypeStruct((n, width), BF16),
        in_specs=[vmem, vmem, vmem],
        out_specs=anywhere,
        scratch_shapes=[pltpu.VMEM((12, n // 8, half), BF16), dma((12,)), dma((1,))],
        compiler_params=pltpu.CompilerParams(vmem_limit_bytes=40 * 2**20),
        name="mix",
    )(combine, gathered, begun)


def solution(mesh):
    in_specs = (P(("seq", "exp"), None), P(), P(), P("exp", None, "seq"), P("exp", "seq", None))
    out_specs = P(("seq", "exp"), None)
    return jax.shard_map(
        on_device, mesh=mesh, in_specs=in_specs, out_specs=out_specs, check_vma=False
    )
```

```python
import functools

import jax
import jax.numpy as jnp
from jax import lax
from jax.experimental import pallas as pl
from jax.experimental.pallas import tpu as pltpu
from jax.sharding import PartitionSpec as P

MESH = pl.DeviceIdType.MESH
F32 = jnp.float32
BF16 = jnp.bfloat16
PLANE = 16
COLUMN = 8
META = 128


RING = (0, 1, 2, 1)


def plane_hops(k):
    return RING[(k >> 3 & 1) * 2 + (k & 1)] + RING[k >> 1 & 3]


def column_hops(k):
    return RING[(k & 1) * 2] + RING[k >> 1 & 3]


def split3(v):
    hi = v.astype(BF16).astype(F32)
    rest = v - hi
    mid = rest.astype(BF16).astype(F32)
    return hi, mid, rest - mid


def meta_block(peak, total):
    rows = peak.shape[0]
    lane = lax.broadcasted_iota(jnp.int32, (rows, META), 1)
    out = jnp.zeros((rows, META), F32)
    for i, part in enumerate(split3(peak) + split3(total)):
        out = jnp.where(lane == i, part, out)
    return out.astype(BF16)


def read_meta(block):
    v = block.astype(F32)
    peak = v[:, 0:1] + v[:, 1:2] + v[:, 2:3]
    total = v[:, 3:4] + v[:, 4:5] + v[:, 5:6]
    return peak, total


def moe_kernel(
    tok, gain_hbm, slot_hbm, win_hbm, wout_hbm,
    cbuf, g_ref, begun,
    raw, xbuf, pair, lbuf, dbuf, win, wout, gain_ref, slot_ref, mx, acc, colbuf,
    s0, r0, s1, r1, s2, r2, sl, hbuf, xs, xr, s4, r4,
    tsem, wsem,
    core_send, core_recv, plane_send, plane_recv, column_send, column_recv,
    back_send, back_recv, gather_send, gather_recv, fwd_send, fwd_recv,
):
    tokens, width = xbuf.shape
    slots = slot_ref.shape[1]
    half = width // 2
    group = sl.shape[1]
    piece = group // 2
    local_experts = win.shape[0]
    per = group // local_experts
    hidden = win.shape[2]
    chunks = tsem.shape[0]
    rows = tokens // chunks

    s = lax.axis_index("seq")
    e = lax.axis_index("exp")
    c = lax.rem(s, 2)
    xh = lax.rem(s // 2, 2)
    z0 = lax.rem(s // 4, 2)
    z1 = s // 8
    xl = lax.rem(e, 2)
    y0 = lax.rem(e // 2, 2)
    y1 = e // 4

    def bit(b, k, i):
        return 1 - b if (k >> i) & 1 else b

    def plane_peer(k):
        pe = (bit(y1, k, 2) * 2 + bit(y0, k, 1)) * 2 + bit(xl, k, 0)
        ph = bit(xh, k, 3)
        ps = ((z1 * 2 + z0) * 2 + ph) * 2 + c
        row = pl.multiple_of(pe * group + ph * piece, piece)
        return (ps, pe), row

    def column_peer(k):
        ph = bit(xh, k, 0)
        ps = ((bit(z1, k, 2) * 2 + bit(z0, k, 1)) * 2 + ph) * 2 + c
        return (ps, e), pl.multiple_of(ph * piece, piece)

    partner = (s + 1 - 2 * c, e)

    def remote(src, dst, send, recv, device):
        return pltpu.make_async_remote_copy(
            src_ref=src, dst_ref=dst, send_sem=send, recv_sem=recv,
            device_id=device, device_id_type=MESH,
        )

    def token_copy(i):
        at = pl.ds(pl.multiple_of(i * rows, rows), rows)
        return pltpu.make_async_copy(tok.at[at], raw.at[at], tsem.at[i])

    gain_copy = pltpu.make_async_copy(gain_hbm, gain_ref, wsem.at[2])
    slot_copy = pltpu.make_async_copy(slot_hbm, slot_ref, wsem.at[3])
    gain_copy.start()
    token_copy(0).start()
    slot_copy.start()
    for i in range(1, chunks):
        token_copy(i).start()
    barrier = pltpu.get_barrier_semaphore()
    greeted = [partner]
    greeted += [plane_peer(k)[0] for k in range(1, PLANE)]
    greeted += [column_peer(k)[0] for k in range(2, COLUMN)]
    for device in greeted:
        pl.semaphore_signal(barrier, inc=1, device_id=device, device_id_type=MESH)
    win_copy = pltpu.make_async_copy(win_hbm, win, wsem.at[0])
    wout_copy = pltpu.make_async_copy(wout_hbm, wout, wsem.at[1])

    gain_copy.wait()
    gain = gain_ref[...]
    mx[...] = jnp.full(mx.shape, -jnp.inf, F32)

    def norm(i, slot):
        for q in range(rows // 32):
            at = pl.ds(pl.multiple_of(i * rows + q * 32, 32), 32)
            v = raw[at, :].astype(F32)
            scale = lax.rsqrt(jnp.mean(v * v, axis=1, keepdims=True) + 1e-06)
            normed = (v * scale * gain).astype(BF16)
            xbuf[at, :] = normed
            pair[slot][q * 32:(q + 1) * 32, :] = normed

    def project_slots(i, slot):
        at = pl.ds(pl.multiple_of(i * rows, rows), rows)
        logits = jnp.dot(pair[slot][...], slot_ref[...], preferred_element_type=F32)
        lbuf[at, :] = logits
        mx[...] = jnp.maximum(mx[...], jnp.max(logits.reshape(rows // 8, 8, slots), axis=0))

    token_copy(0).wait()
    norm(0, 0)
    slot_copy.wait()

    @pl.loop(0, chunks // 2 - 1)
    def _(i):
        token_copy(2 * i + 1).wait()
        token_copy(2 * i + 2).wait()
        for slot in range(2):
            norm(2 * i + slot + 1, 1 - slot)
            project_slots(2 * i + slot, slot)

    token_copy(chunks - 1).wait()
    win_copy.start()
    wout_copy.start()
    norm(chunks - 1, 1)
    project_slots(chunks - 2, 0)
    project_slots(chunks - 1, 1)

    peak = jnp.max(mx[...], axis=0, keepdims=True)

    step = min(256, tokens)

    total = jnp.zeros((8, slots), F32)
    for i in range(tokens // step):
        at = pl.ds(i * step, step)
        ex = jnp.exp(lbuf[at, :] - peak)
        dbuf[at, :] = ex.astype(BF16)
        total += jnp.sum(ex.reshape(step // 8, 8, slots), axis=0)

    total = jnp.sum(total, axis=0, keepdims=True)
    line = lax.broadcasted_iota(jnp.int32, (META, slots), 0)
    both = jnp.where(line == 0, peak, jnp.where(line == 1, total, 0.0))
    colbuf[...] = jnp.transpose(both)
    my_meta = meta_block(colbuf[:, 0:1], colbuf[:, 1:2])

    def weigh(h):
        cols = pl.ds(pl.multiple_of(h * half, half), half)
        return lax.dot_general(
            dbuf[...], xbuf[:, cols], (((0,), (0,)), ((), ())), preferred_element_type=F32
        )

    s0[:, :half] = weigh(1 - c).astype(BF16)
    s0[:, half:] = my_meta
    pl.semaphore_wait(barrier, len(greeted))
    first_copy = remote(s0, r0, core_send.at[0], core_recv.at[0], partner)
    first_copy.start()
    acc[...] = weigh(c)
    first_copy.wait()

    mine, my_total = colbuf[:, 0:1], colbuf[:, 1:2]
    other, other_total = read_meta(r0[:, half:])
    joint = jnp.maximum(mine, other)
    wa, wb = jnp.exp(mine - joint), jnp.exp(other - joint)
    s1[:, half:] = meta_block(joint, my_total * wa + other_total * wb)
    s1[:, :half] = (acc[...] * wa + r0[:, :half].astype(F32) * wb).astype(BF16)

    order = sorted(range(1, PLANE), key=plane_hops, reverse=True)
    plane_copies = {}
    for k in order:
        device, row = plane_peer(k)
        plane_copies[k] = remote(
            s1.at[pl.ds(row, piece)], r1.at[k], plane_send.at[k], plane_recv.at[k], device
        )
        plane_copies[k].start()
    my_row = plane_peer(0)[1]

    @pl.loop(0, tokens // step, unroll=2)
    def _(i):
        at = pl.ds(pl.multiple_of(i * step, step), step)
        v = lbuf[at, :]
        ex = jnp.exp(v - jnp.max(v, axis=1, keepdims=True))
        cbuf[at, :] = (ex * (1.0 / jnp.sum(ex, axis=1, keepdims=True))).astype(BF16)

    def merge(blocks):
        metas = [read_meta(b[:, half:]) for b in blocks]
        joint = functools.reduce(jnp.maximum, [m for m, _ in metas])
        scales = [jnp.exp(m - joint) for m, _ in metas]
        out = sum(b[:, :half].astype(F32) * w for b, w in zip(blocks, scales))
        return out, joint, sum(t * w for (_, t), w in zip(metas, scales))

    for k in order:
        plane_copies[k].wait_recv()
    summed, joint, total_k = merge([s1[pl.ds(my_row, piece), :]] + [r1[k] for k in range(1, PLANE)])
    s2[:, :half] = summed.astype(BF16)
    s2[:, half:] = meta_block(joint, total_k)

    column_order = sorted(range(1, COLUMN), key=column_hops, reverse=True)
    column_copies = {}
    for k in column_order:
        column_copies[k] = remote(
            s2, r2.at[k], column_send.at[k], column_recv.at[k], column_peer(k)[0]
        )
        column_copies[k].start()
    for k in column_order:
        column_copies[k].wait_recv()
    for low in range(2):
        out, _, tot = merge([s2[...] if k == 0 else r2[k] for k in range(low, COLUMN, 2)])
        sl[c, pl.ds(column_peer(low)[1], piece), :] = (out / tot).astype(BF16)
    in_copy = remote(sl.at[c], sl.at[c], core_send.at[1], core_recv.at[1], partner)
    in_copy.start()
    win_copy.wait()
    wout_copy.wait()

    owner = lax.broadcasted_iota(jnp.int32, (group, hidden), 0) // per

    def enter(h, first):
        rows_in = pl.ds(pl.multiple_of(h * half, half), half)
        for x in range(local_experts):
            y = jnp.dot(sl[h], win[x, rows_in, :], preferred_element_type=F32)
            first = jnp.where(owner == x, first + y, first)
        return first

    first = enter(c, jnp.zeros((group, hidden), F32))
    in_copy.wait()
    first = enter(1 - c, first)
    act = 0.5 * first * (1.0 + lax.erf(first * 0.7071067811865476))
    for x in range(local_experts):
        hbuf[:, x * hidden:(x + 1) * hidden] = jnp.where(owner == x, act, 0.0).astype(BF16)

    def project(h):
        cols = pl.ds(pl.multiple_of(h * half, half), half)
        return sum(
            jnp.dot(hbuf[:, x * hidden:(x + 1) * hidden], wout[x, :, cols], preferred_element_type=F32)
            for x in range(local_experts)
        )

    xs[...] = project(1 - c).astype(BF16)
    out_copy = remote(xs, xr, core_send.at[2], core_recv.at[2], partner)
    out_copy.start()
    own = project(c)
    out_copy.wait()
    s4[...] = (own + xr[...].astype(F32)).astype(BF16)
    back_copies = {}
    for k in column_order:
        device, at = column_peer(k)
        back_copies[k] = remote(
            s4.at[pl.ds(at, piece)], r4.at[k], back_send.at[k], back_recv.at[k], device
        )
        back_copies[k].start()
    mine = s4[pl.ds(column_peer(0)[1], piece), :].astype(F32)
    for k in column_order:
        back_copies[k].wait_recv()
    for k in column_order:
        mine += r4[k].astype(F32)
    at = pl.ds(my_row, piece)
    g_ref[c, at, :] = mine.astype(BF16)

    gathers = {}
    for k in order:
        gathers[k] = remote(
            g_ref.at[c, at], g_ref.at[c, at], gather_send.at[k], gather_recv.at[k], plane_peer(k)[0]
        )
        gathers[k].start()
    forwards = []
    for k in [0] + order[::-1]:
        if k:
            gathers[k].wait_recv()
        there = pl.ds(plane_peer(k)[1], piece)
        forwards.append(
            remote(g_ref.at[c, there], g_ref.at[c, there], fwd_send.at[k], fwd_recv.at[k], partner)
        )
        forwards[-1].start()
    early = begun.shape[0] // 2
    for i in range(2):
        at = pl.ds(i * early, early)
        begun[at, :] = jnp.dot(
            cbuf[at, :], g_ref[c], preferred_element_type=F32
        ).astype(BF16)
    for copy in forwards:
        copy.wait()
    for copies in (plane_copies, column_copies, back_copies, gathers):
        for copy in copies.values():
            copy.wait_send()


def mix_kernel(c_ref, g_ref, begun, o_hbm, obuf, sem, begun_sem):
    half = g_ref.shape[2]
    rows = obuf.shape[1]
    blocks = o_hbm.shape[0] // rows
    c = lax.rem(lax.axis_index("seq"), 2)
    mine = pl.ds(pl.multiple_of(c * half, half), half)
    rest = pl.ds(pl.multiple_of((1 - c) * half, half), half)
    early = begun.shape[0]
    copies = [pltpu.make_async_copy(begun, o_hbm.at[pl.ds(0, early), mine], begun_sem.at[0])]
    copies[0].start()
    todo = [(i * rows, 1 - c, rest) for i in range(blocks)]
    todo += [(i * rows, c, mine) for i in range(early // rows, blocks)]
    for i, (row, h, cols) in enumerate(todo):
        at = pl.ds(row, rows)
        obuf[i] = jnp.dot(c_ref[at, :], g_ref[h], preferred_element_type=F32).astype(BF16)
        copies.append(pltpu.make_async_copy(obuf.at[i], o_hbm.at[at, cols], sem.at[i]))
        copies[-1].start()
    for copy in copies:
        copy.wait()


def on_device(tokens, norm_gain, slot_param, w_in, w_out):
    n, width = tokens.shape
    slots = slot_param.shape[1]
    half = width // 2
    group = slots // lax.axis_size("exp")
    piece = group // 2
    hidden = w_in.shape[2]
    chunks = 16
    wide = half + META
    dma = pltpu.SemaphoreType.DMA
    anywhere = pl.BlockSpec(memory_space=pltpu.HBM)
    vmem = pl.BlockSpec(memory_space=pltpu.VMEM)
    combine, gathered, begun = pl.pallas_call(
        moe_kernel,
        out_shape=(
            pltpu.VMEM((n, slots), BF16),
            pltpu.VMEM((2, slots, half), BF16),
            pltpu.VMEM((n // 2, half), BF16),
        ),
        in_specs=[anywhere] * 5,
        out_specs=(vmem, vmem, vmem),
        scratch_shapes=[
            pltpu.VMEM((n, width), BF16),
            pltpu.VMEM((n, width), BF16),
            [pltpu.VMEM((n // chunks, width), BF16)] * 2,
            pltpu.VMEM((n, slots), F32),
            pltpu.VMEM((n, slots), BF16),
            pltpu.VMEM(w_in.shape, BF16),
            pltpu.VMEM(w_out.shape, BF16),
            pltpu.VMEM((1, width), F32),
            pltpu.VMEM((width, slots), BF16),
            pltpu.VMEM((8, slots), F32),
            pltpu.VMEM((slots, half), F32),
            pltpu.VMEM((slots, META), F32),
            pltpu.VMEM((slots, wide), BF16),
            pltpu.VMEM((slots, wide), BF16),
            pltpu.VMEM((slots, wide), BF16),
            pltpu.VMEM((PLANE, piece, wide), BF16),
            pltpu.VMEM((piece, wide), BF16),
            pltpu.VMEM((COLUMN, piece, wide), BF16),
            pltpu.VMEM((2, group, half), BF16),
            pltpu.VMEM((group, w_in.shape[0] * hidden), BF16),
            pltpu.VMEM((group, half), BF16),
            pltpu.VMEM((group, half), BF16),
            pltpu.VMEM((group, half), BF16),
            pltpu.VMEM((COLUMN, piece, half), BF16),
            dma((chunks,)),
            dma((4,)),
            dma((3,)), dma((3,)),
            dma((PLANE,)), dma((PLANE,)),
            dma((COLUMN,)), dma((COLUMN,)),
            dma((COLUMN,)), dma((COLUMN,)),
            dma((PLANE,)), dma((PLANE,)),
            dma((PLANE,)), dma((PLANE,)),
        ],
        compiler_params=pltpu.CompilerParams(
            collective_id=0, has_side_effects=True, vmem_limit_bytes=48 * 2**20
        ),
        name="moe",
    )(
        *(
            pltpu.with_memory_space_constraint(a, pltpu.HBM)
            for a in (tokens, norm_gain.reshape(1, width), slot_param, w_in, w_out)
        )
    )
    return pl.pallas_call(
        mix_kernel,
        out_shape=jax.ShapeDtypeStruct((n, width), BF16),
        in_specs=[vmem, vmem, vmem],
        out_specs=anywhere,
        scratch_shapes=[pltpu.VMEM((12, n // 8, half), BF16), dma((12,)), dma((1,))],
        compiler_params=pltpu.CompilerParams(vmem_limit_bytes=40 * 2**20),
        name="mix",
    )(combine, gathered, begun)


def solution(mesh):
    in_specs = (P(("seq", "exp"), None), P(), P(), P("exp", None, "seq"), P("exp", "seq", None))
    out_specs = P(("seq", "exp"), None)
    return jax.shard_map(
        on_device, mesh=mesh, in_specs=in_specs, out_specs=out_specs, check_vma=False
    )
```

```python
import functools

import jax
import jax.numpy as jnp
from jax import lax
from jax.experimental import pallas as pl
from jax.experimental.pallas import tpu as pltpu
from jax.sharding import PartitionSpec as P

MESH = pl.DeviceIdType.MESH
F32 = jnp.float32
BF16 = jnp.bfloat16
PLANE = 16
COLUMN = 8
META = 128
EARLY = 5


RING = (0, 1, 2, 1)


def plane_hops(k):
    return RING[(k >> 3 & 1) * 2 + (k & 1)] + RING[k >> 1 & 3]


def column_hops(k):
    return RING[(k & 1) * 2] + RING[k >> 1 & 3]


def split3(v):
    hi = v.astype(BF16).astype(F32)
    rest = v - hi
    mid = rest.astype(BF16).astype(F32)
    return hi, mid, rest - mid


def meta_block(peak, total):
    rows = peak.shape[0]
    lane = lax.broadcasted_iota(jnp.int32, (rows, META), 1)
    out = jnp.zeros((rows, META), F32)
    for i, part in enumerate(split3(peak) + split3(total)):
        out = jnp.where(lane == i, part, out)
    return out.astype(BF16)


def read_meta(block):
    v = block.astype(F32)
    peak = v[:, 0:1] + v[:, 1:2] + v[:, 2:3]
    total = v[:, 3:4] + v[:, 4:5] + v[:, 5:6]
    return peak, total


def moe_kernel(
    tok, gain_hbm, slot_hbm, win_hbm, wout_hbm,
    cbuf, g_ref, begun,
    raw, xbuf, pair, lbuf, dbuf, win, wout, gain_ref, slot_ref, mx, acc, colbuf,
    s0, r0, s1, r1, s2, r2, sl, hbuf, xs, xr, s4, r4,
    tsem, wsem,
    core_send, core_recv, plane_send, plane_recv, column_send, column_recv,
    back_send, back_recv, gather_send, gather_recv, fwd_send, fwd_recv,
):
    tokens, width = xbuf.shape
    slots = slot_ref.shape[1]
    half = width // 2
    group = sl.shape[1]
    piece = group // 2
    local_experts = win.shape[0]
    per = group // local_experts
    hidden = win.shape[2]
    chunks = tsem.shape[0]
    rows = tokens // chunks

    s = lax.axis_index("seq")
    e = lax.axis_index("exp")
    c = lax.rem(s, 2)
    xh = lax.rem(s // 2, 2)
    z0 = lax.rem(s // 4, 2)
    z1 = s // 8
    xl = lax.rem(e, 2)
    y0 = lax.rem(e // 2, 2)
    y1 = e // 4

    def bit(b, k, i):
        return 1 - b if (k >> i) & 1 else b

    def plane_peer(k):
        pe = (bit(y1, k, 2) * 2 + bit(y0, k, 1)) * 2 + bit(xl, k, 0)
        ph = bit(xh, k, 3)
        ps = ((z1 * 2 + z0) * 2 + ph) * 2 + c
        row = pl.multiple_of(pe * group + ph * piece, piece)
        return (ps, pe), row

    def column_peer(k):
        ph = bit(xh, k, 0)
        ps = ((bit(z1, k, 2) * 2 + bit(z0, k, 1)) * 2 + ph) * 2 + c
        return (ps, e), pl.multiple_of(ph * piece, piece)

    partner = (s + 1 - 2 * c, e)

    def remote(src, dst, send, recv, device):
        return pltpu.make_async_remote_copy(
            src_ref=src, dst_ref=dst, send_sem=send, recv_sem=recv,
            device_id=device, device_id_type=MESH,
        )

    def token_copy(i):
        at = pl.ds(pl.multiple_of(i * rows, rows), rows)
        return pltpu.make_async_copy(tok.at[at], raw.at[at], tsem.at[i])

    gain_copy = pltpu.make_async_copy(gain_hbm, gain_ref, wsem.at[2])
    slot_copy = pltpu.make_async_copy(slot_hbm, slot_ref, wsem.at[3])
    gain_copy.start()
    token_copy(0).start()
    slot_copy.start()
    for i in range(1, EARLY):
        token_copy(i).start()
    barrier = pltpu.get_barrier_semaphore()
    greeted = [partner]
    greeted += [plane_peer(k)[0] for k in range(1, PLANE)]
    greeted += [column_peer(k)[0] for k in range(2, COLUMN)]
    for device in greeted:
        pl.semaphore_signal(barrier, inc=1, device_id=device, device_id_type=MESH)
    win_copy = pltpu.make_async_copy(win_hbm, win, wsem.at[0])
    wout_copy = pltpu.make_async_copy(wout_hbm, wout, wsem.at[1])

    gain_copy.wait()
    gain = gain_ref[...]
    mx[...] = jnp.full(mx.shape, -jnp.inf, F32)

    def norm(i, slot):
        for q in range(rows // 32):
            at = pl.ds(pl.multiple_of(i * rows + q * 32, 32), 32)
            v = raw[at, :].astype(F32)
            scale = lax.rsqrt(jnp.mean(v * v, axis=1, keepdims=True) + 1e-06)
            normed = (v * scale * gain).astype(BF16)
            xbuf[at, :] = normed
            pair[slot][q * 32:(q + 1) * 32, :] = normed

    def project_slots(i, slot):
        at = pl.ds(pl.multiple_of(i * rows, rows), rows)
        logits = jnp.dot(pair[slot][...], slot_ref[...], preferred_element_type=F32)
        lbuf[at, :] = logits
        mx[...] = jnp.maximum(mx[...], jnp.max(logits.reshape(rows // 8, 8, slots), axis=0))

    token_copy(0).wait()
    for i in range(EARLY, chunks):
        token_copy(i).start()
    norm(0, 0)
    slot_copy.wait()

    @pl.loop(0, chunks // 2 - 1)
    def _(i):
        token_copy(2 * i + 1).wait()
        token_copy(2 * i + 2).wait()
        for slot in range(2):
            norm(2 * i + slot + 1, 1 - slot)
            project_slots(2 * i + slot, slot)

    token_copy(chunks - 1).wait()
    win_copy.start()
    wout_copy.start()
    norm(chunks - 1, 1)
    project_slots(chunks - 2, 0)
    project_slots(chunks - 1, 1)

    peak = jnp.max(mx[...], axis=0, keepdims=True)

    step = min(256, tokens)

    total = jnp.zeros((8, slots), F32)
    for i in range(tokens // step):
        at = pl.ds(i * step, step)
        ex = jnp.exp(lbuf[at, :] - peak)
        dbuf[at, :] = ex.astype(BF16)
        total += jnp.sum(ex.reshape(step // 8, 8, slots), axis=0)

    total = jnp.sum(total, axis=0, keepdims=True)
    line = lax.broadcasted_iota(jnp.int32, (META, slots), 0)
    both = jnp.where(line == 0, peak, jnp.where(line == 1, total, 0.0))
    colbuf[...] = jnp.transpose(both)
    my_meta = meta_block(colbuf[:, 0:1], colbuf[:, 1:2])

    def weigh(h):
        cols = pl.ds(pl.multiple_of(h * half, half), half)
        return lax.dot_general(
            dbuf[...], xbuf[:, cols], (((0,), (0,)), ((), ())), preferred_element_type=F32
        )

    s0[:, :half] = weigh(1 - c).astype(BF16)
    s0[:, half:] = my_meta
    pl.semaphore_wait(barrier, len(greeted))
    first_copy = remote(s0, r0, core_send.at[0], core_recv.at[0], partner)
    first_copy.start()
    acc[...] = weigh(c)
    first_copy.wait()

    mine, my_total = colbuf[:, 0:1], colbuf[:, 1:2]
    other, other_total = read_meta(r0[:, half:])
    joint = jnp.maximum(mine, other)
    wa, wb = jnp.exp(mine - joint), jnp.exp(other - joint)
    s1[:, half:] = meta_block(joint, my_total * wa + other_total * wb)
    s1[:, :half] = (acc[...] * wa + r0[:, :half].astype(F32) * wb).astype(BF16)

    order = sorted(range(1, PLANE), key=plane_hops, reverse=True)
    plane_copies = {}
    for k in order:
        device, row = plane_peer(k)
        plane_copies[k] = remote(
            s1.at[pl.ds(row, piece)], r1.at[k], plane_send.at[k], plane_recv.at[k], device
        )
        plane_copies[k].start()
    my_row = plane_peer(0)[1]

    @pl.loop(0, tokens // step, unroll=2)
    def _(i):
        at = pl.ds(pl.multiple_of(i * step, step), step)
        v = lbuf[at, :]
        ex = jnp.exp(v - jnp.max(v, axis=1, keepdims=True))
        cbuf[at, :] = (ex * (1.0 / jnp.sum(ex, axis=1, keepdims=True))).astype(BF16)

    def merge(blocks):
        metas = [read_meta(b[:, half:]) for b in blocks]
        joint = functools.reduce(jnp.maximum, [m for m, _ in metas])
        scales = [jnp.exp(m - joint) for m, _ in metas]
        out = sum(b[:, :half].astype(F32) * w for b, w in zip(blocks, scales))
        return out, joint, sum(t * w for (_, t), w in zip(metas, scales))

    for k in order:
        plane_copies[k].wait_recv()
    summed, joint, total_k = merge([s1[pl.ds(my_row, piece), :]] + [r1[k] for k in range(1, PLANE)])
    s2[:, :half] = summed.astype(BF16)
    s2[:, half:] = meta_block(joint, total_k)

    column_order = sorted(range(1, COLUMN), key=column_hops, reverse=True)
    column_copies = {}
    for k in column_order:
        column_copies[k] = remote(
            s2, r2.at[k], column_send.at[k], column_recv.at[k], column_peer(k)[0]
        )
        column_copies[k].start()
    for k in column_order:
        column_copies[k].wait_recv()
    for low in range(2):
        out, _, tot = merge([s2[...] if k == 0 else r2[k] for k in range(low, COLUMN, 2)])
        sl[c, pl.ds(column_peer(low)[1], piece), :] = (out / tot).astype(BF16)
    in_copy = remote(sl.at[c], sl.at[c], core_send.at[1], core_recv.at[1], partner)
    in_copy.start()
    win_copy.wait()
    wout_copy.wait()

    owner = lax.broadcasted_iota(jnp.int32, (group, hidden), 0) // per

    def enter(h, first):
        rows_in = pl.ds(pl.multiple_of(h * half, half), half)
        for x in range(local_experts):
            y = jnp.dot(sl[h], win[x, rows_in, :], preferred_element_type=F32)
            first = jnp.where(owner == x, first + y, first)
        return first

    first = enter(c, jnp.zeros((group, hidden), F32))
    in_copy.wait()
    first = enter(1 - c, first)
    act = 0.5 * first * (1.0 + lax.erf(first * 0.7071067811865476))
    for x in range(local_experts):
        hbuf[:, x * hidden:(x + 1) * hidden] = jnp.where(owner == x, act, 0.0).astype(BF16)

    def project(h):
        cols = pl.ds(pl.multiple_of(h * half, half), half)
        return sum(
            jnp.dot(hbuf[:, x * hidden:(x + 1) * hidden], wout[x, :, cols], preferred_element_type=F32)
            for x in range(local_experts)
        )

    xs[...] = project(1 - c).astype(BF16)
    out_copy = remote(xs, xr, core_send.at[2], core_recv.at[2], partner)
    out_copy.start()
    own = project(c)
    out_copy.wait()
    s4[...] = (own + xr[...].astype(F32)).astype(BF16)
    back_copies = {}
    for k in column_order:
        device, at = column_peer(k)
        back_copies[k] = remote(
            s4.at[pl.ds(at, piece)], r4.at[k], back_send.at[k], back_recv.at[k], device
        )
        back_copies[k].start()
    mine = s4[pl.ds(column_peer(0)[1], piece), :].astype(F32)
    for k in column_order:
        back_copies[k].wait_recv()
    for k in column_order:
        mine += r4[k].astype(F32)
    at = pl.ds(my_row, piece)
    g_ref[c, at, :] = mine.astype(BF16)

    gathers = {}
    for k in order:
        gathers[k] = remote(
            g_ref.at[c, at], g_ref.at[c, at], gather_send.at[k], gather_recv.at[k], plane_peer(k)[0]
        )
        gathers[k].start()
    forwards = []
    for k in [0] + order[::-1]:
        if k:
            gathers[k].wait_recv()
        there = pl.ds(plane_peer(k)[1], piece)
        forwards.append(
            remote(g_ref.at[c, there], g_ref.at[c, there], fwd_send.at[k], fwd_recv.at[k], partner)
        )
        forwards[-1].start()
    early = begun.shape[0] // 2
    for i in range(2):
        at = pl.ds(i * early, early)
        begun[at, :] = jnp.dot(
            cbuf[at, :], g_ref[c], preferred_element_type=F32
        ).astype(BF16)
    for copy in forwards:
        copy.wait()
    for copies in (plane_copies, column_copies, back_copies, gathers):
        for copy in copies.values():
            copy.wait_send()


def mix_kernel(c_ref, g_ref, begun, o_hbm, obuf, sem, begun_sem):
    half = g_ref.shape[2]
    rows = obuf.shape[1]
    blocks = o_hbm.shape[0] // rows
    c = lax.rem(lax.axis_index("seq"), 2)
    mine = pl.ds(pl.multiple_of(c * half, half), half)
    rest = pl.ds(pl.multiple_of((1 - c) * half, half), half)
    early = begun.shape[0]
    copies = [pltpu.make_async_copy(begun, o_hbm.at[pl.ds(0, early), mine], begun_sem.at[0])]
    copies[0].start()
    todo = [(i * rows, 1 - c, rest) for i in range(blocks)]
    todo += [(i * rows, c, mine) for i in range(early // rows, blocks)]
    for i, (row, h, cols) in enumerate(todo):
        at = pl.ds(row, rows)
        obuf[i] = jnp.dot(c_ref[at, :], g_ref[h], preferred_element_type=F32).astype(BF16)
        copies.append(pltpu.make_async_copy(obuf.at[i], o_hbm.at[at, cols], sem.at[i]))
        copies[-1].start()
    for copy in copies:
        copy.wait()


def on_device(tokens, norm_gain, slot_param, w_in, w_out):
    n, width = tokens.shape
    slots = slot_param.shape[1]
    half = width // 2
    group = slots // lax.axis_size("exp")
    piece = group // 2
    hidden = w_in.shape[2]
    chunks = 16
    wide = half + META
    dma = pltpu.SemaphoreType.DMA
    anywhere = pl.BlockSpec(memory_space=pltpu.HBM)
    vmem = pl.BlockSpec(memory_space=pltpu.VMEM)
    combine, gathered, begun = pl.pallas_call(
        moe_kernel,
        out_shape=(
            pltpu.VMEM((n, slots), BF16),
            pltpu.VMEM((2, slots, half), BF16),
            pltpu.VMEM((n // 2, half), BF16),
        ),
        in_specs=[anywhere] * 5,
        out_specs=(vmem, vmem, vmem),
        scratch_shapes=[
            pltpu.VMEM((n, width), BF16),
            pltpu.VMEM((n, width), BF16),
            [pltpu.VMEM((n // chunks, width), BF16)] * 2,
            pltpu.VMEM((n, slots), F32),
            pltpu.VMEM((n, slots), BF16),
            pltpu.VMEM(w_in.shape, BF16),
            pltpu.VMEM(w_out.shape, BF16),
            pltpu.VMEM((1, width), F32),
            pltpu.VMEM((width, slots), BF16),
            pltpu.VMEM((8, slots), F32),
            pltpu.VMEM((slots, half), F32),
            pltpu.VMEM((slots, META), F32),
            pltpu.VMEM((slots, wide), BF16),
            pltpu.VMEM((slots, wide), BF16),
            pltpu.VMEM((slots, wide), BF16),
            pltpu.VMEM((PLANE, piece, wide), BF16),
            pltpu.VMEM((piece, wide), BF16),
            pltpu.VMEM((COLUMN, piece, wide), BF16),
            pltpu.VMEM((2, group, half), BF16),
            pltpu.VMEM((group, w_in.shape[0] * hidden), BF16),
            pltpu.VMEM((group, half), BF16),
            pltpu.VMEM((group, half), BF16),
            pltpu.VMEM((group, half), BF16),
            pltpu.VMEM((COLUMN, piece, half), BF16),
            dma((chunks,)),
            dma((4,)),
            dma((3,)), dma((3,)),
            dma((PLANE,)), dma((PLANE,)),
            dma((COLUMN,)), dma((COLUMN,)),
            dma((COLUMN,)), dma((COLUMN,)),
            dma((PLANE,)), dma((PLANE,)),
            dma((PLANE,)), dma((PLANE,)),
        ],
        compiler_params=pltpu.CompilerParams(
            collective_id=0, has_side_effects=True, vmem_limit_bytes=48 * 2**20
        ),
        name="moe",
    )(
        *(
            pltpu.with_memory_space_constraint(a, pltpu.HBM)
            for a in (tokens, norm_gain.reshape(1, width), slot_param, w_in, w_out)
        )
    )
    return pl.pallas_call(
        mix_kernel,
        out_shape=jax.ShapeDtypeStruct((n, width), BF16),
        in_specs=[vmem, vmem, vmem],
        out_specs=anywhere,
        scratch_shapes=[pltpu.VMEM((12, n // 8, half), BF16), dma((12,)), dma((1,))],
        compiler_params=pltpu.CompilerParams(vmem_limit_bytes=40 * 2**20),
        name="mix",
    )(combine, gathered, begun)


def solution(mesh):
    in_specs = (P(("seq", "exp"), None), P(), P(), P("exp", None, "seq"), P("exp", "seq", None))
    out_specs = P(("seq", "exp"), None)
    return jax.shard_map(
        on_device, mesh=mesh, in_specs=in_specs, out_specs=out_specs, check_vma=False
    )
```

```python
import functools

import jax
import jax.numpy as jnp
from jax import lax
from jax.experimental import pallas as pl
from jax.experimental.pallas import tpu as pltpu
from jax.sharding import PartitionSpec as P

MESH = pl.DeviceIdType.MESH
F32 = jnp.float32
BF16 = jnp.bfloat16
PLANE = 16
COLUMN = 8
META = 128
EARLY = 5


RING = (0, 1, 2, 1)


def plane_hops(k):
    return RING[(k >> 3 & 1) * 2 + (k & 1)] + RING[k >> 1 & 3]


def column_hops(k):
    return RING[(k & 1) * 2] + RING[k >> 1 & 3]


def split3(v):
    hi = v.astype(BF16).astype(F32)
    rest = v - hi
    mid = rest.astype(BF16).astype(F32)
    return hi, mid, rest - mid


def meta_block(peak, total):
    lane = lax.broadcasted_iota(jnp.int32, peak.shape, 1)
    out = jnp.zeros(peak.shape, F32)
    for i, part in enumerate(split3(peak) + split3(total)):
        out = jnp.where(lane == i, part, out)
    return out.astype(BF16)


def read_meta(block):
    row = lax.broadcasted_iota(jnp.int32, (META, 2 * META), 0) // 3
    column = lax.broadcasted_iota(jnp.int32, (META, 2 * META), 1) // META
    pick = jnp.where(row == column, 1.0, 0.0).astype(BF16)
    both = jnp.dot(block, pick, preferred_element_type=F32)
    return both[:, :META], both[:, META:]


def wide(v, width):
    return jnp.concatenate([v] * (width // META), axis=1)


def moe_kernel(
    tok, gain_hbm, slot_hbm, win_hbm, wout_hbm,
    cbuf, g_ref, begun,
    raw, xbuf, pair, lbuf, dbuf, win, wout, gain_ref, slot_ref, mx, acc, colbuf,
    s0, r0, s1, r1, s2, r2, sl, hbuf, xs, xr, s4, r4,
    tsem, wsem,
    core_send, core_recv, plane_send, plane_recv, column_send, column_recv,
    back_send, back_recv, gather_send, gather_recv, fwd_send, fwd_recv,
):
    tokens, width = xbuf.shape
    slots = slot_ref.shape[1]
    half = width // 2
    group = sl.shape[1]
    piece = group // 2
    local_experts = win.shape[0]
    per = group // local_experts
    hidden = win.shape[2]
    chunks = tsem.shape[0]
    rows = tokens // chunks

    s = lax.axis_index("seq")
    e = lax.axis_index("exp")
    c = lax.rem(s, 2)
    xh = lax.rem(s // 2, 2)
    z0 = lax.rem(s // 4, 2)
    z1 = s // 8
    xl = lax.rem(e, 2)
    y0 = lax.rem(e // 2, 2)
    y1 = e // 4

    def bit(b, k, i):
        return 1 - b if (k >> i) & 1 else b

    def plane_peer(k):
        pe = (bit(y1, k, 2) * 2 + bit(y0, k, 1)) * 2 + bit(xl, k, 0)
        ph = bit(xh, k, 3)
        ps = ((z1 * 2 + z0) * 2 + ph) * 2 + c
        row = pl.multiple_of(pe * group + ph * piece, piece)
        return (ps, pe), row

    def column_peer(k):
        ph = bit(xh, k, 0)
        ps = ((bit(z1, k, 2) * 2 + bit(z0, k, 1)) * 2 + ph) * 2 + c
        return (ps, e), pl.multiple_of(ph * piece, piece)

    partner = (s + 1 - 2 * c, e)

    def remote(src, dst, send, recv, device):
        return pltpu.make_async_remote_copy(
            src_ref=src, dst_ref=dst, send_sem=send, recv_sem=recv,
            device_id=device, device_id_type=MESH,
        )

    def token_copy(i):
        at = pl.ds(pl.multiple_of(i * rows, rows), rows)
        return pltpu.make_async_copy(tok.at[at], raw.at[at], tsem.at[i])

    gain_copy = pltpu.make_async_copy(gain_hbm, gain_ref, wsem.at[2])
    slot_copy = pltpu.make_async_copy(slot_hbm, slot_ref, wsem.at[3])
    gain_copy.start()
    token_copy(0).start()
    slot_copy.start()
    for i in range(1, EARLY):
        token_copy(i).start()
    barrier = pltpu.get_barrier_semaphore()
    greeted = [partner]
    greeted += [plane_peer(k)[0] for k in range(1, PLANE)]
    greeted += [column_peer(k)[0] for k in range(2, COLUMN)]
    for device in greeted:
        pl.semaphore_signal(barrier, inc=1, device_id=device, device_id_type=MESH)
    win_copy = pltpu.make_async_copy(win_hbm, win, wsem.at[0])
    wout_copy = pltpu.make_async_copy(wout_hbm, wout, wsem.at[1])

    gain_copy.wait()
    gain = gain_ref[...]
    mx[...] = jnp.full(mx.shape, -jnp.inf, F32)

    def norm(i, slot):
        for q in range(rows // 32):
            at = pl.ds(pl.multiple_of(i * rows + q * 32, 32), 32)
            v = raw[at, :].astype(F32)
            scale = lax.rsqrt(jnp.mean(v * v, axis=1, keepdims=True) + 1e-06)
            normed = (v * scale * gain).astype(BF16)
            xbuf[at, :] = normed
            pair[slot][q * 32:(q + 1) * 32, :] = normed

    def project_slots(i, slot):
        at = pl.ds(pl.multiple_of(i * rows, rows), rows)
        logits = jnp.dot(pair[slot][...], slot_ref[...], preferred_element_type=F32)
        lbuf[at, :] = logits
        mx[...] = jnp.maximum(mx[...], jnp.max(logits.reshape(rows // 8, 8, slots), axis=0))

    token_copy(0).wait()
    for i in range(EARLY, chunks):
        token_copy(i).start()
    norm(0, 0)
    slot_copy.wait()

    @pl.loop(0, chunks // 2 - 1)
    def _(i):
        token_copy(2 * i + 1).wait()
        token_copy(2 * i + 2).wait()
        for slot in range(2):
            norm(2 * i + slot + 1, 1 - slot)
            project_slots(2 * i + slot, slot)

    token_copy(chunks - 1).wait()
    win_copy.start()
    wout_copy.start()
    norm(chunks - 1, 1)
    project_slots(chunks - 2, 0)
    project_slots(chunks - 1, 1)

    peak = jnp.max(mx[...], axis=0, keepdims=True)

    step = min(256, tokens)

    total = jnp.zeros((8, slots), F32)
    for i in range(tokens // step):
        at = pl.ds(i * step, step)
        ex = jnp.exp(lbuf[at, :] - peak)
        dbuf[at, :] = ex.astype(BF16)
        total += jnp.sum(ex.reshape(step // 8, 8, slots), axis=0)

    total = jnp.sum(total, axis=0, keepdims=True)
    colbuf[0] = jnp.transpose(jnp.broadcast_to(peak, (META, slots)))
    colbuf[1] = jnp.transpose(jnp.broadcast_to(total, (META, slots)))
    my_meta = meta_block(colbuf[0], colbuf[1])

    def weigh(h):
        cols = pl.ds(pl.multiple_of(h * half, half), half)
        return lax.dot_general(
            dbuf[...], xbuf[:, cols], (((0,), (0,)), ((), ())), preferred_element_type=F32
        )

    s0[:, :half] = weigh(1 - c).astype(BF16)
    s0[:, half:] = my_meta
    pl.semaphore_wait(barrier, len(greeted))
    first_copy = remote(s0, r0, core_send.at[0], core_recv.at[0], partner)
    first_copy.start()
    acc[...] = weigh(c)
    first_copy.wait()

    mine, my_total = colbuf[0], colbuf[1]
    other, other_total = read_meta(r0[:, half:])
    joint = jnp.maximum(mine, other)
    wa, wb = jnp.exp(mine - joint), jnp.exp(other - joint)
    s1[:, half:] = meta_block(joint, my_total * wa + other_total * wb)
    s1[:, :half] = (
        acc[...] * wide(wa, half) + r0[:, :half].astype(F32) * wide(wb, half)
    ).astype(BF16)

    order = sorted(range(1, PLANE), key=plane_hops, reverse=True)
    plane_copies = {}
    for k in order:
        device, row = plane_peer(k)
        plane_copies[k] = remote(
            s1.at[pl.ds(row, piece)], r1.at[k], plane_send.at[k], plane_recv.at[k], device
        )
        plane_copies[k].start()
    my_row = plane_peer(0)[1]

    @pl.loop(0, tokens // step, unroll=2)
    def _(i):
        at = pl.ds(pl.multiple_of(i * step, step), step)
        v = lbuf[at, :]
        ex = jnp.exp(v - jnp.max(v, axis=1, keepdims=True))
        cbuf[at, :] = (ex * (1.0 / jnp.sum(ex, axis=1, keepdims=True))).astype(BF16)

    def merge(blocks):
        peaks, totals = read_meta(jnp.concatenate([b[:, half:] for b in blocks], axis=0))
        cut = [slice(i * piece, (i + 1) * piece) for i in range(len(blocks))]
        joint = functools.reduce(jnp.maximum, [peaks[at] for at in cut])
        scales = [jnp.exp(peaks[at] - joint) for at in cut]
        out = sum(b[:, :half].astype(F32) * wide(w, half) for b, w in zip(blocks, scales))
        return out, joint, sum(totals[at] * w for at, w in zip(cut, scales))

    for k in order:
        plane_copies[k].wait_recv()
    summed, joint, total_k = merge([s1[pl.ds(my_row, piece), :]] + [r1[k] for k in range(1, PLANE)])
    s2[:, :half] = summed.astype(BF16)
    s2[:, half:] = meta_block(joint, total_k)

    column_order = sorted(range(1, COLUMN), key=column_hops, reverse=True)
    column_copies = {}
    for k in column_order:
        column_copies[k] = remote(
            s2, r2.at[k], column_send.at[k], column_recv.at[k], column_peer(k)[0]
        )
        column_copies[k].start()
    for copy in plane_copies.values():
        copy.wait_send()
    for k in column_order:
        column_copies[k].wait_recv()
    for low in range(2):
        out, _, tot = merge([s2[...] if k == 0 else r2[k] for k in range(low, COLUMN, 2)])
        sl[c, pl.ds(column_peer(low)[1], piece), :] = (out / wide(tot, half)).astype(BF16)
    in_copy = remote(sl.at[c], sl.at[c], core_send.at[1], core_recv.at[1], partner)
    in_copy.start()
    win_copy.wait()
    wout_copy.wait()

    owner = lax.broadcasted_iota(jnp.int32, (group, hidden), 0) // per

    def enter(h, first):
        rows_in = pl.ds(pl.multiple_of(h * half, half), half)
        for x in range(local_experts):
            y = jnp.dot(sl[h], win[x, rows_in, :], preferred_element_type=F32)
            first = jnp.where(owner == x, first + y, first)
        return first

    first = enter(c, jnp.zeros((group, hidden), F32))
    in_copy.wait()
    first = enter(1 - c, first)
    act = 0.5 * first * (1.0 + lax.erf(first * 0.7071067811865476))
    for x in range(local_experts):
        hbuf[:, x * hidden:(x + 1) * hidden] = jnp.where(owner == x, act, 0.0).astype(BF16)

    def project(h):
        cols = pl.ds(pl.multiple_of(h * half, half), half)
        return sum(
            jnp.dot(hbuf[:, x * hidden:(x + 1) * hidden], wout[x, :, cols], preferred_element_type=F32)
            for x in range(local_experts)
        )

    xs[...] = project(1 - c).astype(BF16)
    out_copy = remote(xs, xr, core_send.at[2], core_recv.at[2], partner)
    out_copy.start()
    own = project(c)
    out_copy.wait()
    s4[...] = (own + xr[...].astype(F32)).astype(BF16)
    back_copies = {}
    for k in column_order:
        device, at = column_peer(k)
        back_copies[k] = remote(
            s4.at[pl.ds(at, piece)], r4.at[k], back_send.at[k], back_recv.at[k], device
        )
        back_copies[k].start()
    mine = s4[pl.ds(column_peer(0)[1], piece), :].astype(F32)
    for copy in column_copies.values():
        copy.wait_send()
    for k in column_order:
        back_copies[k].wait_recv()
    for k in column_order:
        mine += r4[k].astype(F32)
    at = pl.ds(my_row, piece)
    g_ref[c, at, :] = mine.astype(BF16)

    gathers = {}
    for k in order:
        gathers[k] = remote(
            g_ref.at[c, at], g_ref.at[c, at], gather_send.at[k], gather_recv.at[k], plane_peer(k)[0]
        )
        gathers[k].start()
    for copy in back_copies.values():
        copy.wait_send()
    forwards = []
    for k in [0] + order[::-1]:
        if k:
            gathers[k].wait_recv()
        there = pl.ds(plane_peer(k)[1], piece)
        forwards.append(
            remote(g_ref.at[c, there], g_ref.at[c, there], fwd_send.at[k], fwd_recv.at[k], partner)
        )
        forwards[-1].start()
    early = begun.shape[0] // 2
    for i in range(2):
        at = pl.ds(i * early, early)
        begun[at, :] = jnp.dot(
            cbuf[at, :], g_ref[c], preferred_element_type=F32
        ).astype(BF16)
    for copy in gathers.values():
        copy.wait_send()
    for copy in forwards:
        copy.wait()


def mix_kernel(c_ref, g_ref, begun, o_hbm, obuf, sem, begun_sem):
    half = g_ref.shape[2]
    rows = obuf.shape[1]
    blocks = o_hbm.shape[0] // rows
    c = lax.rem(lax.axis_index("seq"), 2)
    mine = pl.ds(pl.multiple_of(c * half, half), half)
    rest = pl.ds(pl.multiple_of((1 - c) * half, half), half)
    early = begun.shape[0]
    copies = [pltpu.make_async_copy(begun, o_hbm.at[pl.ds(0, early), mine], begun_sem.at[0])]
    copies[0].start()
    todo = [(i * rows, 1 - c, rest) for i in range(blocks)]
    todo += [(i * rows, c, mine) for i in range(early // rows, blocks)]
    for i, (row, h, cols) in enumerate(todo):
        at = pl.ds(row, rows)
        obuf[i] = jnp.dot(c_ref[at, :], g_ref[h], preferred_element_type=F32).astype(BF16)
        copies.append(pltpu.make_async_copy(obuf.at[i], o_hbm.at[at, cols], sem.at[i]))
        copies[-1].start()
    for copy in copies:
        copy.wait()


def on_device(tokens, norm_gain, slot_param, w_in, w_out):
    n, width = tokens.shape
    slots = slot_param.shape[1]
    half = width // 2
    group = slots // lax.axis_size("exp")
    piece = group // 2
    hidden = w_in.shape[2]
    chunks = 16
    wide = half + META
    dma = pltpu.SemaphoreType.DMA
    anywhere = pl.BlockSpec(memory_space=pltpu.HBM)
    vmem = pl.BlockSpec(memory_space=pltpu.VMEM)
    combine, gathered, begun = pl.pallas_call(
        moe_kernel,
        out_shape=(
            pltpu.VMEM((n, slots), BF16),
            pltpu.VMEM((2, slots, half), BF16),
            pltpu.VMEM((n // 2, half), BF16),
        ),
        in_specs=[anywhere] * 5,
        out_specs=(vmem, vmem, vmem),
        scratch_shapes=[
            pltpu.VMEM((n, width), BF16),
            pltpu.VMEM((n, width), BF16),
            [pltpu.VMEM((n // chunks, width), BF16)] * 2,
            pltpu.VMEM((n, slots), F32),
            pltpu.VMEM((n, slots), BF16),
            pltpu.VMEM(w_in.shape, BF16),
            pltpu.VMEM(w_out.shape, BF16),
            pltpu.VMEM((1, width), F32),
            pltpu.VMEM((width, slots), BF16),
            pltpu.VMEM((8, slots), F32),
            pltpu.VMEM((slots, half), F32),
            pltpu.VMEM((2, slots, META), F32),
            pltpu.VMEM((slots, wide), BF16),
            pltpu.VMEM((slots, wide), BF16),
            pltpu.VMEM((slots, wide), BF16),
            pltpu.VMEM((PLANE, piece, wide), BF16),
            pltpu.VMEM((piece, wide), BF16),
            pltpu.VMEM((COLUMN, piece, wide), BF16),
            pltpu.VMEM((2, group, half), BF16),
            pltpu.VMEM((group, w_in.shape[0] * hidden), BF16),
            pltpu.VMEM((group, half), BF16),
            pltpu.VMEM((group, half), BF16),
            pltpu.VMEM((group, half), BF16),
            pltpu.VMEM((COLUMN, piece, half), BF16),
            dma((chunks,)),
            dma((4,)),
            dma((3,)), dma((3,)),
            dma((PLANE,)), dma((PLANE,)),
            dma((COLUMN,)), dma((COLUMN,)),
            dma((COLUMN,)), dma((COLUMN,)),
            dma((PLANE,)), dma((PLANE,)),
            dma((PLANE,)), dma((PLANE,)),
        ],
        compiler_params=pltpu.CompilerParams(
            collective_id=0, has_side_effects=True, vmem_limit_bytes=48 * 2**20
        ),
        name="moe",
    )(
        *(
            pltpu.with_memory_space_constraint(a, pltpu.HBM)
            for a in (tokens, norm_gain.reshape(1, width), slot_param, w_in, w_out)
        )
    )
    return pl.pallas_call(
        mix_kernel,
        out_shape=jax.ShapeDtypeStruct((n, width), BF16),
        in_specs=[vmem, vmem, vmem],
        out_specs=anywhere,
        scratch_shapes=[pltpu.VMEM((12, n // 8, half), BF16), dma((12,)), dma((1,))],
        compiler_params=pltpu.CompilerParams(vmem_limit_bytes=40 * 2**20),
        name="mix",
    )(combine, gathered, begun)


def solution(mesh):
    in_specs = (P(("seq", "exp"), None), P(), P(), P("exp", None, "seq"), P("exp", "seq", None))
    out_specs = P(("seq", "exp"), None)
    return jax.shard_map(
        on_device, mesh=mesh, in_specs=in_specs, out_specs=out_specs, check_vma=False
    )
```

```python
import functools

import jax
import jax.numpy as jnp
from jax import lax
from jax.experimental import pallas as pl
from jax.experimental.pallas import tpu as pltpu
from jax.sharding import PartitionSpec as P

MESH = pl.DeviceIdType.MESH
F32 = jnp.float32
BF16 = jnp.bfloat16
PLANE = 16
COLUMN = 8
META = 128
EARLY = 5


RING = (0, 1, 2, 1)


def plane_hops(k):
    return RING[(k >> 3 & 1) * 2 + (k & 1)] + RING[k >> 1 & 3]


def column_hops(k):
    return RING[(k & 1) * 2] + RING[k >> 1 & 3]


def split3(v):
    hi = v.astype(BF16).astype(F32)
    rest = v - hi
    mid = rest.astype(BF16).astype(F32)
    return hi, mid, rest - mid


def meta_block(peak, total):
    lane = lax.broadcasted_iota(jnp.int32, peak.shape, 1)
    out = jnp.zeros(peak.shape, F32)
    for i, part in enumerate(split3(peak) + split3(total)):
        out = jnp.where(lane == i, part, out)
    return out.astype(BF16)


def read_meta(block):
    row = lax.broadcasted_iota(jnp.int32, (META, 2 * META), 0) // 3
    column = lax.broadcasted_iota(jnp.int32, (META, 2 * META), 1) // META
    pick = jnp.where(row == column, 1.0, 0.0).astype(BF16)
    both = jnp.dot(block, pick, preferred_element_type=F32)
    return both[:, :META], both[:, META:]


def wide(v, width):
    return jnp.concatenate([v] * (width // META), axis=1)


def moe_kernel(
    tok, gain_hbm, slot_hbm, win_hbm, wout_hbm,
    cbuf, g_ref, begun,
    raw, xbuf, pair, lbuf, dbuf, win, wout, gain_ref, slot_ref, mx, acc, colbuf,
    s0, r0, s1, r1, s2, r2, sl, hbuf, xs, xr, s4, r4,
    tsem, wsem,
    core_send, core_recv, plane_send, plane_recv, column_send, column_recv,
    back_send, back_recv, gather_send, gather_recv, fwd_send, fwd_recv,
):
    tokens, width = xbuf.shape
    slots = slot_ref.shape[1]
    half = width // 2
    group = sl.shape[1]
    piece = group // 2
    local_experts = win.shape[0]
    per = group // local_experts
    hidden = win.shape[2]
    chunks = tsem.shape[0]
    rows = tokens // chunks

    s = lax.axis_index("seq")
    e = lax.axis_index("exp")
    c = lax.rem(s, 2)
    xh = lax.rem(s // 2, 2)
    z0 = lax.rem(s // 4, 2)
    z1 = s // 8
    xl = lax.rem(e, 2)
    y0 = lax.rem(e // 2, 2)
    y1 = e // 4

    def bit(b, k, i):
        return 1 - b if (k >> i) & 1 else b

    def plane_peer(k):
        pe = (bit(y1, k, 2) * 2 + bit(y0, k, 1)) * 2 + bit(xl, k, 0)
        ph = bit(xh, k, 3)
        ps = ((z1 * 2 + z0) * 2 + ph) * 2 + c
        row = pl.multiple_of(pe * group + ph * piece, piece)
        return (ps, pe), row

    def column_peer(k):
        ph = bit(xh, k, 0)
        ps = ((bit(z1, k, 2) * 2 + bit(z0, k, 1)) * 2 + ph) * 2 + c
        return (ps, e), pl.multiple_of(ph * piece, piece)

    partner = (s + 1 - 2 * c, e)

    def remote(src, dst, send, recv, device):
        return pltpu.make_async_remote_copy(
            src_ref=src, dst_ref=dst, send_sem=send, recv_sem=recv,
            device_id=device, device_id_type=MESH,
        )

    def token_copy(i):
        at = pl.ds(pl.multiple_of(i * rows, rows), rows)
        return pltpu.make_async_copy(tok.at[at], raw.at[at], tsem.at[i])

    gain_copy = pltpu.make_async_copy(gain_hbm, gain_ref, wsem.at[2])
    slot_copy = pltpu.make_async_copy(slot_hbm, slot_ref, wsem.at[3])
    gain_copy.start()
    token_copy(0).start()
    slot_copy.start()
    for i in range(1, EARLY):
        token_copy(i).start()
    barrier = pltpu.get_barrier_semaphore()
    greeted = [partner]
    greeted += [plane_peer(k)[0] for k in range(1, PLANE)]
    greeted += [column_peer(k)[0] for k in range(2, COLUMN)]
    for device in greeted:
        pl.semaphore_signal(barrier, inc=1, device_id=device, device_id_type=MESH)
    win_copy = pltpu.make_async_copy(win_hbm, win, wsem.at[0])
    wout_copy = pltpu.make_async_copy(wout_hbm, wout, wsem.at[1])

    gain_copy.wait()
    gain = gain_ref[...]
    mx[...] = jnp.full(mx.shape, -jnp.inf, F32)

    def norm(i, slot):
        for q in range(rows // 32):
            at = pl.ds(pl.multiple_of(i * rows + q * 32, 32), 32)
            v = raw[at, :].astype(F32)
            scale = lax.rsqrt(jnp.mean(v * v, axis=1, keepdims=True) + 1e-06)
            normed = (v * scale * gain).astype(BF16)
            xbuf[at, :] = normed
            pair[slot][q * 32:(q + 1) * 32, :] = normed

    def project_slots(i, slot):
        at = pl.ds(pl.multiple_of(i * rows, rows), rows)
        logits = jnp.dot(pair[slot][...], slot_ref[...], preferred_element_type=F32)
        lbuf[at, :] = logits
        mx[...] = jnp.maximum(mx[...], jnp.max(logits.reshape(rows // 8, 8, slots), axis=0))

    token_copy(0).wait()
    for i in range(EARLY, chunks):
        token_copy(i).start()
    norm(0, 0)
    slot_copy.wait()

    @pl.loop(0, chunks // 2 - 1)
    def _(i):
        token_copy(2 * i + 1).wait()
        token_copy(2 * i + 2).wait()
        for slot in range(2):
            norm(2 * i + slot + 1, 1 - slot)
            project_slots(2 * i + slot, slot)

    token_copy(chunks - 1).wait()
    win_copy.start()
    wout_copy.start()
    norm(chunks - 1, 1)
    project_slots(chunks - 2, 0)
    project_slots(chunks - 1, 1)

    peak = jnp.max(mx[...], axis=0, keepdims=True)

    step = min(256, tokens)

    total = jnp.zeros((8, slots), F32)
    for i in range(tokens // step):
        at = pl.ds(i * step, step)
        ex = jnp.exp(lbuf[at, :] - peak)
        dbuf[at, :] = ex.astype(BF16)
        total += jnp.sum(ex.reshape(step // 8, 8, slots), axis=0)

    total = jnp.sum(total, axis=0, keepdims=True)
    colbuf[0] = jnp.transpose(jnp.broadcast_to(peak, (META, slots)))
    colbuf[1] = jnp.transpose(jnp.broadcast_to(total, (META, slots)))
    my_meta = meta_block(colbuf[0], colbuf[1])

    def weigh(h):
        cols = pl.ds(pl.multiple_of(h * half, half), half)
        return lax.dot_general(
            dbuf[...], xbuf[:, cols], (((0,), (0,)), ((), ())), preferred_element_type=F32
        )

    s0[:, :half] = weigh(1 - c).astype(BF16)
    s0[:, half:] = my_meta
    pl.semaphore_wait(barrier, len(greeted))
    first_copy = remote(s0, r0, core_send.at[0], core_recv.at[0], partner)
    first_copy.start()
    acc[...] = weigh(c)
    first_copy.wait()

    mine, my_total = colbuf[0], colbuf[1]
    other, other_total = read_meta(r0[:, half:])
    joint = jnp.maximum(mine, other)
    wa, wb = jnp.exp(mine - joint), jnp.exp(other - joint)
    s1[:, half:] = meta_block(joint, my_total * wa + other_total * wb)
    s1[:, :half] = (
        acc[...] * wide(wa, half) + r0[:, :half].astype(F32) * wide(wb, half)
    ).astype(BF16)

    order = sorted(range(1, PLANE), key=plane_hops, reverse=True)
    plane_copies = {}
    for k in order:
        device, row = plane_peer(k)
        plane_copies[k] = remote(
            s1.at[pl.ds(row, piece)], r1.at[k], plane_send.at[k], plane_recv.at[k], device
        )
        plane_copies[k].start()
    my_row = plane_peer(0)[1]

    @pl.loop(0, tokens // step, unroll=2)
    def _(i):
        at = pl.ds(pl.multiple_of(i * step, step), step)
        v = lbuf[at, :]
        ex = jnp.exp(v - jnp.max(v, axis=1, keepdims=True))
        cbuf[at, :] = (ex * (1.0 / jnp.sum(ex, axis=1, keepdims=True))).astype(BF16)

    def merge(blocks):
        peaks, totals = read_meta(jnp.concatenate([b[:, half:] for b in blocks], axis=0))
        cut = [slice(i * piece, (i + 1) * piece) for i in range(len(blocks))]
        joint = functools.reduce(jnp.maximum, [peaks[at] for at in cut])
        scales = [jnp.exp(peaks[at] - joint) for at in cut]
        out = sum(b[:, :half].astype(F32) * wide(w, half) for b, w in zip(blocks, scales))
        return out, joint, sum(totals[at] * w for at, w in zip(cut, scales))

    for k in order[::-1]:
        plane_copies[k].wait_recv()
    summed, joint, total_k = merge([s1[pl.ds(my_row, piece), :]] + [r1[k] for k in range(1, PLANE)])
    s2[:, :half] = summed.astype(BF16)
    s2[:, half:] = meta_block(joint, total_k)

    column_order = sorted(range(1, COLUMN), key=column_hops, reverse=True)
    column_copies = {}
    for k in column_order:
        column_copies[k] = remote(
            s2, r2.at[k], column_send.at[k], column_recv.at[k], column_peer(k)[0]
        )
        column_copies[k].start()
    for copy in plane_copies.values():
        copy.wait_send()
    for k in column_order[::-1]:
        column_copies[k].wait_recv()
    for low in range(2):
        out, _, tot = merge([s2[...] if k == 0 else r2[k] for k in range(low, COLUMN, 2)])
        sl[c, pl.ds(column_peer(low)[1], piece), :] = (out / wide(tot, half)).astype(BF16)
    in_copy = remote(sl.at[c], sl.at[c], core_send.at[1], core_recv.at[1], partner)
    in_copy.start()
    win_copy.wait()
    wout_copy.wait()

    owner = lax.broadcasted_iota(jnp.int32, (group, hidden), 0) // per

    def enter(h, first):
        rows_in = pl.ds(pl.multiple_of(h * half, half), half)
        for x in range(local_experts):
            y = jnp.dot(sl[h], win[x, rows_in, :], preferred_element_type=F32)
            first = jnp.where(owner == x, first + y, first)
        return first

    first = enter(c, jnp.zeros((group, hidden), F32))
    in_copy.wait()
    first = enter(1 - c, first)
    act = 0.5 * first * (1.0 + lax.erf(first * 0.7071067811865476))
    for x in range(local_experts):
        hbuf[:, x * hidden:(x + 1) * hidden] = jnp.where(owner == x, act, 0.0).astype(BF16)

    def project(h):
        cols = pl.ds(pl.multiple_of(h * half, half), half)
        return sum(
            jnp.dot(hbuf[:, x * hidden:(x + 1) * hidden], wout[x, :, cols], preferred_element_type=F32)
            for x in range(local_experts)
        )

    xs[...] = project(1 - c).astype(BF16)
    out_copy = remote(xs, xr, core_send.at[2], core_recv.at[2], partner)
    out_copy.start()
    own = project(c)
    out_copy.wait()
    s4[...] = (own + xr[...].astype(F32)).astype(BF16)
    back_copies = {}
    for k in column_order:
        device, at = column_peer(k)
        back_copies[k] = remote(
            s4.at[pl.ds(at, piece)], r4.at[k], back_send.at[k], back_recv.at[k], device
        )
        back_copies[k].start()
    mine = s4[pl.ds(column_peer(0)[1], piece), :].astype(F32)
    for copy in column_copies.values():
        copy.wait_send()
    for k in column_order[::-1]:
        back_copies[k].wait_recv()
    for k in column_order:
        mine += r4[k].astype(F32)
    at = pl.ds(my_row, piece)
    g_ref[c, at, :] = mine.astype(BF16)

    gathers = {}
    for k in order:
        gathers[k] = remote(
            g_ref.at[c, at], g_ref.at[c, at], gather_send.at[k], gather_recv.at[k], plane_peer(k)[0]
        )
        gathers[k].start()
    for copy in back_copies.values():
        copy.wait_send()
    forwards = []
    for k in [0] + order[::-1]:
        if k:
            gathers[k].wait_recv()
        there = pl.ds(plane_peer(k)[1], piece)
        forwards.append(
            remote(g_ref.at[c, there], g_ref.at[c, there], fwd_send.at[k], fwd_recv.at[k], partner)
        )
        forwards[-1].start()
    early = begun.shape[0] // 2
    for i in range(2):
        at = pl.ds(i * early, early)
        begun[at, :] = jnp.dot(
            cbuf[at, :], g_ref[c], preferred_element_type=F32
        ).astype(BF16)
    for copy in gathers.values():
        copy.wait_send()
    for copy in forwards:
        copy.wait()


def mix_kernel(c_ref, g_ref, begun, o_hbm, obuf, sem, begun_sem):
    half = g_ref.shape[2]
    rows = obuf.shape[1]
    blocks = o_hbm.shape[0] // rows
    c = lax.rem(lax.axis_index("seq"), 2)
    mine = pl.ds(pl.multiple_of(c * half, half), half)
    rest = pl.ds(pl.multiple_of((1 - c) * half, half), half)
    early = begun.shape[0]
    copies = [pltpu.make_async_copy(begun, o_hbm.at[pl.ds(0, early), mine], begun_sem.at[0])]
    copies[0].start()
    todo = [(i * rows, 1 - c, rest) for i in range(blocks)]
    todo += [(i * rows, c, mine) for i in range(early // rows, blocks)]
    for i, (row, h, cols) in enumerate(todo):
        at = pl.ds(row, rows)
        obuf[i] = jnp.dot(c_ref[at, :], g_ref[h], preferred_element_type=F32).astype(BF16)
        copies.append(pltpu.make_async_copy(obuf.at[i], o_hbm.at[at, cols], sem.at[i]))
        copies[-1].start()
    for copy in copies:
        copy.wait()


def on_device(tokens, norm_gain, slot_param, w_in, w_out):
    n, width = tokens.shape
    slots = slot_param.shape[1]
    half = width // 2
    group = slots // lax.axis_size("exp")
    piece = group // 2
    hidden = w_in.shape[2]
    chunks = 16
    wide = half + META
    dma = pltpu.SemaphoreType.DMA
    anywhere = pl.BlockSpec(memory_space=pltpu.HBM)
    vmem = pl.BlockSpec(memory_space=pltpu.VMEM)
    combine, gathered, begun = pl.pallas_call(
        moe_kernel,
        out_shape=(
            pltpu.VMEM((n, slots), BF16),
            pltpu.VMEM((2, slots, half), BF16),
            pltpu.VMEM((n // 2, half), BF16),
        ),
        in_specs=[anywhere] * 5,
        out_specs=(vmem, vmem, vmem),
        scratch_shapes=[
            pltpu.VMEM((n, width), BF16),
            pltpu.VMEM((n, width), BF16),
            [pltpu.VMEM((n // chunks, width), BF16)] * 2,
            pltpu.VMEM((n, slots), F32),
            pltpu.VMEM((n, slots), BF16),
            pltpu.VMEM(w_in.shape, BF16),
            pltpu.VMEM(w_out.shape, BF16),
            pltpu.VMEM((1, width), F32),
            pltpu.VMEM((width, slots), BF16),
            pltpu.VMEM((8, slots), F32),
            pltpu.VMEM((slots, half), F32),
            pltpu.VMEM((2, slots, META), F32),
            pltpu.VMEM((slots, wide), BF16),
            pltpu.VMEM((slots, wide), BF16),
            pltpu.VMEM((slots, wide), BF16),
            pltpu.VMEM((PLANE, piece, wide), BF16),
            pltpu.VMEM((piece, wide), BF16),
            pltpu.VMEM((COLUMN, piece, wide), BF16),
            pltpu.VMEM((2, group, half), BF16),
            pltpu.VMEM((group, w_in.shape[0] * hidden), BF16),
            pltpu.VMEM((group, half), BF16),
            pltpu.VMEM((group, half), BF16),
            pltpu.VMEM((group, half), BF16),
            pltpu.VMEM((COLUMN, piece, half), BF16),
            dma((chunks,)),
            dma((4,)),
            dma((3,)), dma((3,)),
            dma((PLANE,)), dma((PLANE,)),
            dma((COLUMN,)), dma((COLUMN,)),
            dma((COLUMN,)), dma((COLUMN,)),
            dma((PLANE,)), dma((PLANE,)),
            dma((PLANE,)), dma((PLANE,)),
        ],
        compiler_params=pltpu.CompilerParams(
            collective_id=0, has_side_effects=True, vmem_limit_bytes=48 * 2**20
        ),
        name="moe",
    )(
        *(
            pltpu.with_memory_space_constraint(a, pltpu.HBM)
            for a in (tokens, norm_gain.reshape(1, width), slot_param, w_in, w_out)
        )
    )
    return pl.pallas_call(
        mix_kernel,
        out_shape=jax.ShapeDtypeStruct((n, width), BF16),
        in_specs=[vmem, vmem, vmem],
        out_specs=anywhere,
        scratch_shapes=[pltpu.VMEM((12, n // 8, half), BF16), dma((12,)), dma((1,))],
        compiler_params=pltpu.CompilerParams(vmem_limit_bytes=40 * 2**20),
        name="mix",
    )(combine, gathered, begun)


def solution(mesh):
    in_specs = (P(("seq", "exp"), None), P(), P(), P("exp", None, "seq"), P("exp", "seq", None))
    out_specs = P(("seq", "exp"), None)
    return jax.shard_map(
        on_device, mesh=mesh, in_specs=in_specs, out_specs=out_specs, check_vma=False
    )
```
